128 devices in a mesh: seg: 4 (over x), exp: 32 (over z, y, core).
Axes of the slice: x: 4, y: 4, z: 4, core: 2. Of those that a mesh axis runs over, the one named last changes fastest.
Arguments:
- images: float32 [32, 2048, 4096], P('exp', 'seg'), may hold values from -6 to 6
- psf_coef: float32 [32, 2, 3], P('exp'), may hold values from 0.2 to 1
- phases: int32 [32, 2], P('exp'), may hold values from 0 to 15
- col_shift: int32 [32], P('exp'), may hold values from -40 to 40
- band_offset: int32 [32], P('exp'), may hold values from 0 to 16
- exposure_weight: bfloat16 [32], P('exp'), may hold values from 0.5 to 4
- patch_site: int32 [160], replicated, may hold values from 0 to 159, each once
Outputs:
- coadded: float32 [160, 32, 2048], P('exp', 'seg')
The draws below stay inside these ranges and needn't reach their ends.
Inputs may be any that keep to these rules, and one draw needn't show every extreme that they name: `phases`: a phase index p moves the sampling point by p / 16 of a pixel, the first entry along rows, the second along columns. An exposure's pixel column j lands on sky column j + col_shift. An exposure covers the sky bands band_offset to band_offset + 2048 / 32 - 1. `patch_site`: every sky position 2 * band + half is the site of exactly one stored patch.
All inputs are finite; a program needn't handle non-finite values.
Results may differ from the reference program's by a relative error of at most 0.0029.
Values may be sent and summed in bfloat16 or wider, within the bound.
A program may use at most 128 MiB of HBM per device.

```python
import math
import jax
import jax.numpy as jnp
from jax import lax

W = 4096
BAND_ROWS = 32
SEG_BANDS = 16
TAPS = 21
NBASIS = 3
PHASES = 16
DXMAX = 40
EXPOSURES = 32
CCD_ROWS = 2048
SKY_BANDS = 80
PATCHES = 160
N_SEG = 4


def touch_ends(drawn, stream_key, smallest, high):
    extent = drawn.shape
    index_at = [jax.random.randint(jax.random.fold_in(stream_key, axis), (), 0, extent[axis]) for axis in range(len(extent))]
    drawn = drawn.at[tuple(index_at)].set(smallest)
    longest = extent.index(max(extent))
    index_at[longest] = (index_at[longest] + 1) % extent[longest]
    return drawn.at[tuple(index_at)].set(high)


def levels(stream_key, shape, split, least, high):
    def one(axis_at, shards_of):
        draws = jax.random.uniform(jax.random.fold_in(jax.random.fold_in(stream_key, 6), axis_at), (shards_of,), jnp.float32, least / len(split), high / len(split))
        return jnp.repeat(jnp.exp(draws), shape[axis_at] // shards_of).reshape((-1,) + (1,) * (len(shape) - axis_at - 1))

    gain = one(*split[0])
    for cut in split[1:]:
        gain = gain * one(*cut)
    return gain


def scatter_about(rng, extent, scale, most, split=(), dtype=jnp.bfloat16):
    level = levels(rng, extent, split, -0.22, 0.18) if split else 1.0
    drawn = jax.random.normal(rng, extent, jnp.float32) * scale * level
    return jnp.minimum(jnp.maximum(drawn, -most), most).astype(dtype)


def setup_inputs(seed: int = 0) -> dict:
    key_list = jax.random.split(jax.random.key(seed), 8)
    return {
        "images": scatter_about(key_list[0], (EXPOSURES, CCD_ROWS, W), 1.0, 6.0, ((0, 32), (1, 4)), jnp.float32),
        "psf_coef": jnp.clip(jnp.exp(math.log(1.0) - 1.609438 * jax.random.uniform(key_list[1], (EXPOSURES, 2, NBASIS), jnp.float32) ** levels(key_list[1], (EXPOSURES, 2, NBASIS), ((0, 32),), -0.2, 0.2)), 0.2, 1.0),
        "phases": touch_ends(jax.random.randint(key_list[2], (EXPOSURES, 2), 0, PHASES), jax.random.fold_in(key_list[2], 1), 0, PHASES - 1).astype(jnp.int32),
        "col_shift": touch_ends(jax.random.randint(key_list[3], (EXPOSURES,), 0 - DXMAX, DXMAX + 1), jax.random.fold_in(key_list[3], 1), 0 - DXMAX, DXMAX).astype(jnp.int32),
        "band_offset": touch_ends(jax.random.randint(key_list[4], (EXPOSURES,), 0, SKY_BANDS - N_SEG * SEG_BANDS + 1), jax.random.fold_in(key_list[4], 1), 0, SKY_BANDS - N_SEG * SEG_BANDS).astype(jnp.int32),
        "exposure_weight": jnp.clip(jnp.exp(math.log(4.0) - 2.0794415 * jax.random.uniform(key_list[5], (EXPOSURES,), jnp.float32) ** levels(key_list[5], (EXPOSURES,), ((0, 32),), -0.2, 0.2)), 0.5, 4.0).astype(jnp.bfloat16),
        "patch_site": jax.random.permutation(key_list[6], PATCHES).astype(jnp.int32),
    }


sigmas = (1.0, 2.0, 3.5)


def basis_table():
    offsets = jnp.arange(TAPS).astype(jnp.float32) - (TAPS // 2)
    table_rows = []
    for spread in sigmas:
        curve = jnp.exp(-offsets * offsets / (2.0 * spread * spread))
        table_rows.append(curve / jnp.sum(curve))
    return jnp.stack(table_rows)


def lanczos_weights(phase):
    fraction = phase.astype(jnp.float32) / PHASES
    offsets = jnp.arange(6).astype(jnp.float32) - 2.0
    shifted = offsets - fraction
    values = jnp.sinc(shifted) * jnp.sinc(shifted / 3.0)
    return values / jnp.sum(values)


def convolve(source, kernel, before, after, axis):
    length_axis = source.shape[axis]
    padding = [(0, 0), (0, 0)]
    padding[axis] = (before, after)
    padded = jnp.pad(source, padding)
    total = jnp.zeros(source.shape, jnp.float32)
    for position in range(kernel.shape[0]):
        total = total + kernel[position] * lax.slice_in_dim(padded, position, position + length_axis, axis=axis)
    return total


def warp_one(exposure, coef_pair, phase_pair, shift):
    basis_rows = basis_table()
    kernel_rows = jnp.sum(coef_pair[0][:, None] * basis_rows, axis=0)
    kernel_cols = jnp.sum(coef_pair[1][:, None] * basis_rows, axis=0)
    reach = TAPS // 2
    matched = convolve(exposure, kernel_rows, reach, reach, 0)
    matched = convolve(matched, kernel_cols, reach, reach, 1)
    shift_rows = lanczos_weights(phase_pair[0])
    shift_cols = lanczos_weights(phase_pair[1])
    along_rows = convolve(matched, shift_rows, 2, 3, 0)
    count_cols = exposure.shape[1]
    padded = jnp.pad(along_rows, ((0, 0), (DXMAX + 2, DXMAX + 3)))
    total = jnp.zeros(exposure.shape, jnp.float32)
    for position in range(6):
        row_start = (position + DXMAX - shift).astype(jnp.int32)
        total = total + shift_cols[position] * lax.dynamic_slice_in_dim(padded, row_start, count_cols, 1)
    return total


def reference(images, psf_coef, phases, col_shift, band_offset, exposure_weight, patch_site):
    count_cols = images.shape[2]
    half_cols = count_cols // 2
    columns = jnp.arange(count_cols).astype(jnp.int32)

    def add_exposure(state_pair, inputs):
        sky_sum, weight_sum = state_pair
        exposure, coef_pair, phase_pair, shift, offset, scale_weight = inputs
        warped = warp_one(exposure, coef_pair, phase_pair, shift)
        sent_rows = (scale_weight.astype(jnp.float32) * warped).astype(jnp.bfloat16)
        sent_rows = lax.optimization_barrier(sent_rows)
        inside = (columns - shift >= 0) & (columns - shift < count_cols)
        coverage = jnp.where(inside, scale_weight, jnp.zeros((), jnp.bfloat16))
        anchor = jnp.zeros((), jnp.int32)
        row_start = (offset * BAND_ROWS).astype(jnp.int32)
        sky_block = lax.dynamic_slice(sky_sum, (row_start, anchor), (CCD_ROWS, count_cols))
        sky_sum = lax.dynamic_update_slice(sky_sum, sky_block + sent_rows.astype(jnp.float32), (row_start, anchor))
        band_start = offset.astype(jnp.int32)
        band_block = lax.dynamic_slice(weight_sum, (band_start, anchor), (CCD_ROWS // BAND_ROWS, count_cols))
        weight_sum = lax.dynamic_update_slice(weight_sum, band_block + coverage.astype(jnp.float32)[None, :], (band_start, anchor))
        return (sky_sum, weight_sum), None

    sky_start = jnp.zeros((SKY_BANDS * BAND_ROWS, count_cols), jnp.float32)
    weight_start = jnp.zeros((SKY_BANDS, count_cols), jnp.float32)
    (sky_sum, weight_sum), _ = lax.scan(add_exposure, (sky_start, weight_start),
                                        (images, psf_coef, phases, col_shift, band_offset, exposure_weight))
    sky_sum = sky_sum.reshape(SKY_BANDS, BAND_ROWS, 2, half_cols).transpose(0, 2, 1, 3).reshape(PATCHES, BAND_ROWS, half_cols)
    weight_sum = weight_sum.reshape(PATCHES, half_cols)
    picked = jnp.take(sky_sum, patch_site, axis=0)
    totals = jnp.take(weight_sum, patch_site, axis=0)
    return picked / jnp.maximum(totals, 1.0)[:, None, :]
```

```python
import functools
import numpy as np
import jax
import jax.numpy as jnp
from jax import lax
from jax.experimental import pallas as pl
from jax.experimental.pallas import tpu as pltpu
from jax.sharding import PartitionSpec as P

MESH = pl.DeviceIdType.MESH
BF = jnp.bfloat16
F32 = jnp.float32
I32 = jnp.int32
TAPS = 21
SIGMAS = (1.0, 2.0, 3.5)
HALO = 16
ROWS = 512
COLS = 4096
EXT = ROWS + 2 * HALO
PADC = 128


def basis_numbers():
    u = np.arange(TAPS, dtype=np.float64) - TAPS // 2
    out = []
    for s in SIGMAS:
        g = np.exp(-u * u / (2.0 * s * s))
        out.append(g / g.sum())
    return np.stack(out)


def lanczos_table():
    rows = []
    for p in range(16):
        u = np.arange(6, dtype=np.float64) - 2.0 - p / 16.0
        v = np.sinc(u) * np.sinc(u / 3.0)
        rows.append(v / v.sum())
    return np.stack(rows).astype(np.float32)


BASIS = basis_numbers()


def here():
    s = lax.axis_index("seg")
    e = lax.axis_index("exp")
    return s, e // 8, (e // 2) % 4, e % 2


def exp_index(z, y, c):
    return (z * 4 + y) * 2 + c


def banded(shape, distance, numbers):
    out = jnp.zeros(shape, F32)
    for t, number in enumerate(numbers):
        out = jnp.where(distance == t, number, out)
    return out


def split(v):
    high = v.astype(BF)
    return high, (v - high.astype(F32)).astype(BF)


def dot(a, b):
    return jnp.dot(a, b, preferred_element_type=F32)


def exact_dot(a, b):
    return jnp.dot(a, b, precision=lax.Precision.HIGHEST, preferred_element_type=F32)


def taps_of(coef, axis):
    return [
        coef[0, axis, 0] * F32(BASIS[0, t])
        + coef[0, axis, 1] * F32(BASIS[1, t])
        + coef[0, axis, 2] * F32(BASIS[2, t])
        for t in range(TAPS)
    ]


def build_columns(coef, table, phases, shift_ref, chi, clo):
    shift = shift_ref[0]
    kc = taps_of(coef, 1)
    phase = phases[0, 1]
    lz = [table[phase * 6 + n] for n in range(6)]
    k = lax.broadcasted_iota(I32, (512, 384), 0)
    m = lax.broadcasted_iota(I32, (512, 384), 1)
    inner = banded((512, 384), k - m - 54, kc)
    m = lax.broadcasted_iota(I32, (384, 256), 0)
    j = lax.broadcasted_iota(I32, (384, 256), 1)
    outer = banded((384, 256), m - j - 62 + shift, lz)
    for variant in range(3):
        part = outer
        if variant == 0:
            part = jnp.where(m >= 64, outer, 0.0)
        if variant == 2:
            part = jnp.where(m < 320, outer, 0.0)
        high, low = split(exact_dot(inner, part))
        chi[variant] = high
        clo[variant] = low


def build_rows(s, coef, table, phases, rhi, rlo):
    kr = taps_of(coef, 0)
    phase = phases[0, 0]
    lz = [table[phase * 6 + n] for n in range(6)]
    o = lax.broadcasted_iota(I32, (128, 144), 0)
    m = lax.broadcasted_iota(I32, (128, 144), 1)
    row = (o // 32) * 32 + ((o // 4) % 4) * 8 + ((o // 16) % 2) * 4 + o % 4
    outer = banded((128, 144), m - 6 - row, lz)
    m = lax.broadcasted_iota(I32, (144, 160), 0)
    k = lax.broadcasted_iota(I32, (144, 160), 1)
    inner = banded((144, 160), k - m + 2, kr)
    for block in range(4):
        place = s * ROWS + 128 * block - 8 + m
        part = jnp.where((place >= 0) & (place < 4 * ROWS), inner, 0.0)
        high, low = split(exact_dot(outer, part))
        rhi[block] = high
        rlo[block] = low


def warp_kernel(
    image, coef, phases, table, shift_ref, offset_ref, weight_ref,
    sent, meta,
    xf, xhi, xlo, chi, clo, rhi, rlo,
    load_sem, halo_send, halo_recv, meta_send, meta_recv,
):
    s, z, y, c = here()
    chunks = 4
    loads = []
    for i in range(chunks):
        rows = pl.ds(i * (ROWS // chunks), ROWS // chunks)
        cp = pltpu.make_async_copy(
            image.at[0, rows], xf.at[pl.ds(HALO + i * (ROWS // chunks), ROWS // chunks)], load_sem.at[i]
        )
        cp.start()
        loads.append(cp)
    mine = c * 16 + z * 4 + y
    lane = lax.broadcasted_iota(I32, (8, 128), 1)
    scaled = (weight_ref[0] * 256.0).astype(I32)
    meta[mine] = jnp.where(
        lane == 0, offset_ref[0], jnp.where(lane == 1, shift_ref[0], scaled)
    )

    barrier = pltpu.get_barrier_semaphore()
    up, down = {"seg": (s + 1) % 4}, {"seg": (s + 3) % 4}
    ypeers = [{"exp": exp_index(z, (y + d) % 4, c)} for d in (1, 2, 3)]
    zpeers = [{"exp": exp_index((z + d) % 4, y, c)} for d in (1, 2, 3)]
    partner = {"exp": exp_index(z, y, 1 - c)}
    everyone = [up, down] + ypeers + zpeers + [partner]
    for peer in everyone:
        pl.semaphore_signal(barrier, inc=1, device_id=peer, device_id_type=MESH)
    pl.semaphore_wait(barrier, len(everyone))

    def remote(src, dst, send, recv, peer):
        return pltpu.make_async_remote_copy(
            src_ref=src, dst_ref=dst, send_sem=send, recv_sem=recv, device_id=peer, device_id_type=MESH
        )

    halos = [
        remote(image.at[0, pl.ds(ROWS - HALO, HALO)], xf.at[pl.ds(0, HALO)], halo_send.at[0], halo_recv.at[0], up),
        remote(image.at[0, pl.ds(0, HALO)], xf.at[pl.ds(HALO + ROWS, HALO)], halo_send.at[1], halo_recv.at[1], down),
    ]
    for cp in halos:
        cp.start()

    build_columns(coef, table, phases, shift_ref, chi, clo)
    own = meta.at[mine]
    step = [remote(own, own, meta_send.at[i], meta_recv.at[i], ypeers[i]) for i in range(3)]
    for cp in step:
        cp.start()
    build_rows(s, coef, table, phases, rhi, rlo)
    for side in (0, PADC + COLS):
        xhi[:, side : side + PADC] = jnp.zeros((EXT, PADC), BF)
        xlo[:, side : side + PADC] = jnp.zeros((EXT, PADC), BF)
    for cp in step:
        cp.wait()
    group = meta.at[pl.ds(c * 16 + z * 4, 4)]
    step = [remote(group, group, meta_send.at[3 + i], meta_recv.at[3 + i], zpeers[i]) for i in range(3)]
    for cp in step:
        cp.start()

    def convert(start, count, keep=None):
        rows = pl.ds(start, count)
        value = xf[rows, :]
        if keep is not None:
            value = jnp.where(keep, value, 0.0)
        high, low = split(value)
        xhi[rows, PADC : PADC + COLS] = high
        xlo[rows, PADC : PADC + COLS] = low

    for i in range(chunks):
        loads[i].wait()

        @pl.loop(0, ROWS // chunks // 16)
        def _(t):
            convert(pl.multiple_of(HALO + i * (ROWS // chunks) + t * 16, 16), 16)

    for cp in step:
        cp.wait()
    half = meta.at[pl.ds(c * 16, 16)]
    last = remote(half, half, meta_send.at[6], meta_recv.at[6], partner)
    last.start()
    for cp in halos:
        cp.wait()
    convert(0, HALO, s > 0)
    convert(HALO + ROWS, HALO, s < 3)

    weight = weight_ref[0]

    @pl.loop(0, 16)
    def _(j):
        variant = jnp.where(j == 0, 0, jnp.where(j == 15, 2, 1))
        window = pl.ds(pl.multiple_of(j * 256, 256), 512)
        left = xhi[:, window]
        high, low = chi[variant], clo[variant]
        middle = dot(left, high) + dot(left, low) + dot(xlo[:, window], high)
        mhi, mlo = split(middle)
        half_index = j // 8
        for block in range(4):
            rows = slice(128 * block, 128 * block + 160)
            a, b = mhi[rows], mlo[rows]
            rh, rl = rhi[block], rlo[block]
            out = (dot(rh, a) + dot(rl, a) + dot(rh, b)) * weight
            out = out.astype(BF)
            for side in range(2):
                cb = (j % 8) * 2 + side
                slot = jnp.where(half_index == 0, cb, (cb % 4) * 4 + cb // 4)
                sent[half_index, slot, 4 * block : 4 * block + 4] = out[:, 128 * side : 128 * side + 128].reshape(
                    4, 2, 16, 128
                )

    last.wait()


def warp_call(images, psf_coef, phases, col_shift, band_offset, weight):
    smem = pl.BlockSpec(memory_space=pltpu.SMEM)
    vmem = pl.BlockSpec(memory_space=pltpu.VMEM)
    dma = pltpu.SemaphoreType.DMA
    return pl.pallas_call(
        warp_kernel,
        out_shape=(
            jax.ShapeDtypeStruct((2, 16, 16, 2, 16, 128), BF),
            jax.ShapeDtypeStruct((32, 8, 128), I32),
        ),
        in_specs=[pl.BlockSpec(memory_space=pl.ANY)] + [smem] * 6,
        out_specs=(vmem, vmem),
        scratch_shapes=[
            pltpu.VMEM((EXT, COLS), F32),
            pltpu.VMEM((EXT, COLS + 2 * PADC), BF),
            pltpu.VMEM((EXT, COLS + 2 * PADC), BF),
            pltpu.VMEM((3, 512, 256), BF),
            pltpu.VMEM((3, 512, 256), BF),
            pltpu.VMEM((4, 128, 160), BF),
            pltpu.VMEM((4, 128, 160), BF),
            dma((4,)), dma((2,)), dma((2,)), dma((7,)), dma((7,)),
        ],
        compiler_params=pltpu.CompilerParams(
            collective_id=0, has_side_effects=True, vmem_limit_bytes=60 << 20
        ),
        name="warp",
    )(images, psf_coef, phases, jnp.asarray(lanczos_table().reshape(-1)), col_shift, band_offset, weight)


def per_device(images, psf_coef, phases, col_shift, band_offset, exposure_weight, patch_site):
    sent, meta = warp_call(images, psf_coef, phases, col_shift, band_offset, exposure_weight.astype(F32))
    s = lax.axis_index("seg")
    a = sent[0].reshape(16, 16, 2, 4, 4, 128)
    b = sent[1].reshape(4, 4, 16, 2, 4, 4, 128).transpose(1, 0, 2, 3, 4, 5, 6).reshape(16, 16, 2, 4, 4, 128)
    grid = jnp.stack([a, b]).transpose(2, 4, 3, 5, 0, 1, 6).reshape(16, 4, 8, 2, 2048)
    count_cols, half_cols, segment_count, owner_count = 4096, 2048, 4, 32
    offset_cols = col_shift[0]
    scale_weight = exposure_weight[0]
    columns = jnp.arange(count_cols, dtype=jnp.int32)
    inside_cols = (columns - offset_cols >= 0) & (columns - offset_cols < count_cols)
    coverage = jnp.where(inside_cols, scale_weight, jnp.zeros((), BF)).reshape(2, half_cols)
    site_band = patch_site // 2
    site_half = patch_site % 2
    nothing = jnp.zeros((), BF)
    chosen_cover = jnp.where(site_half[:, None] == 1, coverage[1][None, :], coverage[0][None, :])
    local_band = site_band - band_offset[0] - s * 16
    present = (local_band >= 0) & (local_band < 16)
    safe_band = jnp.clip(local_band, 0, 15)
    quarters = jnp.arange(4)[:, None]
    pieces = grid[safe_band[None, :], quarters, :, site_half[None, :], :]
    pieces = jnp.where(present[None, :, None, None], pieces, nothing)
    pieces = pieces.reshape(128, 5, 8, half_cols)
    covers = jnp.where(present[:, None], chosen_cover, nothing)
    covers = jnp.broadcast_to(covers[None], (4, 160, half_cols)).reshape(128, 5, half_cols)
    pieces = lax.all_to_all(pieces, ("seg", "exp"), split_axis=0, concat_axis=0, tiled=True)
    covers = lax.all_to_all(covers, ("seg", "exp"), split_axis=0, concat_axis=0, tiled=True)
    totals = jnp.sum(pieces, axis=0, dtype=F32)
    weights = jnp.sum(covers, axis=0, dtype=F32)
    return totals / jnp.maximum(weights, 1.0)[:, None, :]


def solution(mesh):
    placed = (P("exp", "seg", None), P("exp", None, None), P("exp", None), P("exp"), P("exp"), P("exp"), P())
    return jax.shard_map(per_device, mesh=mesh, in_specs=placed, out_specs=P("exp", "seg", None), check_vma=False)
```

```python
import functools
import numpy as np
import jax
import jax.numpy as jnp
from jax import lax
from jax.experimental import pallas as pl
from jax.experimental.pallas import tpu as pltpu
from jax.sharding import PartitionSpec as P

MESH = pl.DeviceIdType.MESH
BF = jnp.bfloat16
F32 = jnp.float32
I32 = jnp.int32
TAPS = 21
SIGMAS = (1.0, 2.0, 3.5)
HALO = 16
ROWS = 512
COLS = 4096
EXT = ROWS + 2 * HALO
PADC = 128


def basis_numbers():
    u = np.arange(TAPS, dtype=np.float64) - TAPS // 2
    out = []
    for s in SIGMAS:
        g = np.exp(-u * u / (2.0 * s * s))
        out.append(g / g.sum())
    return np.stack(out)


def lanczos_table():
    rows = []
    for p in range(16):
        u = np.arange(6, dtype=np.float64) - 2.0 - p / 16.0
        v = np.sinc(u) * np.sinc(u / 3.0)
        rows.append(v / v.sum())
    return np.stack(rows).astype(np.float32)


BASIS = basis_numbers()


def here():
    s = lax.axis_index("seg")
    e = lax.axis_index("exp")
    return s, e // 8, (e // 2) % 4, e % 2


def exp_index(z, y, c):
    return (z * 4 + y) * 2 + c


def banded(shape, distance, numbers):
    out = jnp.zeros(shape, F32)
    for t, number in enumerate(numbers):
        out = jnp.where(distance == t, number, out)
    return out


def split(v):
    high = v.astype(BF)
    return high, (v - high.astype(F32)).astype(BF)


def dot(a, b):
    return jnp.dot(a, b, preferred_element_type=F32)


def exact_dot(a, b):
    return jnp.dot(a, b, precision=lax.Precision.HIGHEST, preferred_element_type=F32)


def taps_of(coef, axis):
    return [
        coef[0, axis, 0] * F32(BASIS[0, t])
        + coef[0, axis, 1] * F32(BASIS[1, t])
        + coef[0, axis, 2] * F32(BASIS[2, t])
        for t in range(TAPS)
    ]


def build_columns(coef, table, phases, shift_ref, chi, clo):
    shift = shift_ref[0]
    kc = taps_of(coef, 1)
    phase = phases[0, 1]
    lz = [table[phase * 6 + n] for n in range(6)]
    k = lax.broadcasted_iota(I32, (512, 384), 0)
    m = lax.broadcasted_iota(I32, (512, 384), 1)
    inner = banded((512, 384), k - m - 54, kc)
    m = lax.broadcasted_iota(I32, (384, 256), 0)
    j = lax.broadcasted_iota(I32, (384, 256), 1)
    outer = banded((384, 256), m - j - 62 + shift, lz)
    for variant in range(3):
        part = outer
        if variant == 0:
            part = jnp.where(m >= 64, outer, 0.0)
        if variant == 2:
            part = jnp.where(m < 320, outer, 0.0)
        high, low = split(exact_dot(inner, part))
        chi[variant] = high
        clo[variant] = low


def build_rows(s, coef, table, phases, rhi, rlo):
    kr = taps_of(coef, 0)
    phase = phases[0, 0]
    lz = [table[phase * 6 + n] for n in range(6)]
    o = lax.broadcasted_iota(I32, (128, 144), 0)
    m = lax.broadcasted_iota(I32, (128, 144), 1)
    row = (o // 32) * 32 + ((o // 4) % 4) * 8 + ((o // 16) % 2) * 4 + o % 4
    outer = banded((128, 144), m - 6 - row, lz)
    m = lax.broadcasted_iota(I32, (144, 160), 0)
    k = lax.broadcasted_iota(I32, (144, 160), 1)
    inner = banded((144, 160), k - m + 2, kr)
    for block in range(4):
        place = s * ROWS + 128 * block - 8 + m
        part = jnp.where((place >= 0) & (place < 4 * ROWS), inner, 0.0)
        high, low = split(exact_dot(outer, part))
        rhi[block] = high
        rlo[block] = low


ORDER = (2, 1, 3, 0)


def coadd_kernel(
    image, coef, phases, table, shift_ref, offset_ref, weight_ref, sites,
    out,
    xf, xhi, xlo, chi, clo, rhi, rlo, meta, metas, sent, first, partial, second, total, third,
    quarters, planes, divisor, ready, outgoing, incoming,
    load_sem, halo_send, halo_recv, meta_send, meta_recv, meta_load,
    first_send, first_recv, second_send, second_recv, third_send, third_recv,
    x_send, x_recv, last_send, last_recv, own_sem,
):
    s, z, y, c = here()
    e = exp_index(z, y, c)
    chunks = 4
    rows_each = ROWS // chunks
    loads = []
    for i in range(chunks):
        cp = pltpu.make_async_copy(
            image.at[0, pl.ds(i * rows_each, rows_each)],
            xf.at[pl.ds(HALO + i * rows_each, rows_each)],
            load_sem.at[i],
        )
        cp.start()
        loads.append(cp)
    mine = c * 16 + z * 4 + y
    line = lax.broadcasted_iota(I32, (8, 128), 0)
    scaled = (weight_ref[0] * 256.0).astype(I32)
    meta[mine] = jnp.where(line == 0, offset_ref[0], jnp.where(line == 1, shift_ref[0], scaled))

    barrier = pltpu.get_barrier_semaphore()
    xpeers = {d: {"seg": (s + d) % 4} for d in (1, 2, 3)}
    ypeers = {d: {"exp": exp_index(z, (y + d) % 4, c)} for d in (1, 2, 3)}
    zpeers = {d: {"exp": exp_index((z + d) % 4, y, c)} for d in (1, 2, 3)}
    partner = {"exp": exp_index(z, y, 1 - c)}
    for d in (1, 2, 3):
        pl.semaphore_signal(barrier, inc=1, device_id=xpeers[d], device_id_type=MESH)

    @pl.loop(1, 32)
    def _(d):
        pl.semaphore_signal(barrier, inc=1, device_id={"exp": (e + d) % 32}, device_id_type=MESH)

    pl.semaphore_wait(barrier, 34)

    def remote(src, dst, send, recv, peer):
        return pltpu.make_async_remote_copy(
            src_ref=src, dst_ref=dst, send_sem=send, recv_sem=recv, device_id=peer, device_id_type=MESH
        )

    halos = [
        remote(image.at[0, pl.ds(ROWS - HALO, HALO)], xf.at[pl.ds(0, HALO)],
               halo_send.at[0], halo_recv.at[0], xpeers[1]),
        remote(image.at[0, pl.ds(0, HALO)], xf.at[pl.ds(HALO + ROWS, HALO)],
               halo_send.at[1], halo_recv.at[1], xpeers[3]),
    ]
    for cp in halos:
        cp.start()

    build_columns(coef, table, phases, shift_ref, chi, clo)
    own = meta.at[mine]
    step = [remote(own, own, meta_send.at[d - 1], meta_recv.at[d - 1], ypeers[d]) for d in (1, 2, 3)]
    for cp in step:
        cp.start()
    build_rows(s, coef, table, phases, rhi, rlo)
    for side in (0, PADC + COLS):
        xhi[:, side : side + PADC] = jnp.zeros((EXT, PADC), BF)
        xlo[:, side : side + PADC] = jnp.zeros((EXT, PADC), BF)
    for cp in step:
        cp.wait()
    group = meta.at[pl.ds(c * 16 + z * 4, 4)]
    step = [remote(group, group, meta_send.at[2 + d], meta_recv.at[2 + d], zpeers[d]) for d in (1, 2, 3)]
    for cp in step:
        cp.start()

    def convert(start, count, keep=None):
        rows = pl.ds(start, count)
        value = xf[rows, :]
        if keep is not None:
            value = jnp.where(keep, value, 0.0)
        high, low = split(value)
        xhi[rows, PADC : PADC + COLS] = high
        xlo[rows, PADC : PADC + COLS] = low

    for i in range(chunks):
        loads[i].wait()

        @pl.loop(0, rows_each // 16)
        def _(t):
            convert(pl.multiple_of(HALO + i * rows_each + t * 16, 16), 16)

    for cp in step:
        cp.wait()
    half = meta.at[pl.ds(c * 16, 16)]
    metas_copy = pltpu.make_async_copy(half, metas, meta_load)
    metas_copy.start()
    last_meta = remote(half, half, meta_send.at[6], meta_recv.at[6], partner)
    last_meta.start()
    for cp in halos:
        cp.wait()
    convert(0, HALO, s > 0)
    convert(HALO + ROWS, HALO, s < 3)

    weight = weight_ref[0]

    def first_copy(h, d, side, place):
        peers = (ypeers, zpeers)[h]
        return remote(
            sent.at[h, pl.ds(place, 2)], first.at[h, d - 1, pl.ds(side * 2, 2)],
            first_send.at[h, d - 1, side], first_recv.at[h, d - 1, side], peers[d],
        )

    def column_step(h, d, side):
        base = (y, z)[h]
        jh = ((base + d) % 4) * 2 + side
        j = h * 8 + jh
        variant = jnp.where(j == 0, 0, jnp.where(j == 15, 2, 1))
        window = pl.ds(pl.multiple_of(j * 256, 256), 512)
        left = xhi[:, window]
        high, low = chi[variant], clo[variant]
        middle = dot(left, high) + dot(left, low) + dot(xlo[:, window], high)
        mhi, mlo = split(middle)
        for block in range(4):
            rows = slice(128 * block, 128 * block + 160)
            a, b = mhi[rows], mlo[rows]
            rh, rl = rhi[block], rlo[block]
            got = ((dot(rh, a) + dot(rl, a) + dot(rh, b)) * weight).astype(BF)
            for part in range(2):
                sent[h, jh * 2 + part, 4 * block : 4 * block + 4] = got[
                    :, 128 * part : 128 * part + 128
                ].reshape(4, 2, 16, 128)
        return jh * 2

    for d in ORDER:

        @pl.loop(0, 2)
        def _(side, d=d):
            for h in range(2):
                place = column_step(h, d, side)
                if d:
                    first_copy(h, d, side, place).start()

    last_meta.wait()
    metas_copy.wait()

    off = meta[:, 0, :]
    shift = meta[:, 1, :]
    heavy = meta[:, 2, :].astype(F32) * (1.0 / 256.0)
    lane = lax.broadcasted_iota(I32, (32, 128), 1)
    inband = jnp.where((lane >= off) & (lane < off + 64), 1.0, 0.0).T
    for h in range(2):
        block = (4 * y + z, 4 * z + y)[h]
        col = h * 2048 + block * 128 + lane - shift
        cover = jnp.where((col >= 0) & (col < COLS), heavy, 0.0)
        divisor[h] = jnp.maximum(dot(inband.astype(BF), cover.astype(BF)), 1.0)

    for h in range(2):
        for d in (2, 1, 3):
            for side in range(2):
                first_copy(h, d, side, 0).wait()

    def second_copy(h, d, block):
        peers = (zpeers, ypeers)[h]
        return remote(
            partial.at[h, block], second.at[h, d - 1], second_send.at[h, d - 1], second_recv.at[h, d - 1], peers[d]
        )

    for d in ORDER:
        for h in range(2):
            block = ((z, y)[h] + d) % 4
            starts = []
            for k in range(4):
                row = z * 4 + (y + 4 - k) % 4 if h == 0 else ((z + 4 - k) % 4) * 4 + y
                starts.append(metas[row, 0, 0])

            @pl.loop(0, 32, unroll=4)
            def _(band, h=h, block=block, starts=starts):
                acc = jnp.zeros((2, 16, 128), F32)
                for k in range(4):
                    local = band - starts[k]
                    valid = (local >= 0) & (local < 16)
                    at = jnp.clip(local, 0, 15)
                    if k == 0:
                        piece = sent[h, (y, z)[h] * 4 + block, at]
                    else:
                        piece = first[h, k - 1, block, at]
                    acc = acc + jnp.where(valid, piece, jnp.zeros_like(piece)).astype(F32)
                partial[h, block, band] = acc.astype(BF)

            if d:
                second_copy(h, d, block).start()

    for h in range(2):
        for d in (1, 2, 3):
            second_copy(h, d, 0).wait()

    for h in range(2):
        block = (z, y)[h]

        @pl.loop(0, 32, unroll=4)
        def _(band, h=h, block=block):
            acc = partial[h, block, band].astype(F32)
            for k in range(3):
                acc = acc + second[h, k, band].astype(F32)
            total[0, h, band] = acc[0]
            total[1, h, band] = acc[1]

    cp = remote(total.at[1 - c], third, third_send, third_recv, partner)
    cp.start()
    cp.wait()

    @pl.loop(0, 32, unroll=2)
    def _(band):
        a = total[c, 0, band] + third[0, band]
        b = total[c, 1, band] + third[1, band]
        for q in range(4):
            quarters[q, band] = jnp.concatenate([a[4 * q : 4 * q + 4], b[4 * q : 4 * q + 4]], axis=0)

    moves = []
    for d in (2, 1, 3):
        cp = remote(quarters.at[(s + d) % 4], planes.at[s], x_send.at[d - 1], x_recv.at[d - 1], xpeers[d])
        cp.start()
        moves.append(cp)
    planes[s] = quarters[s]
    for cp in moves:
        cp.wait()

    top = line < 4
    for g in range(5):

        @pl.loop(0, 16, unroll=4)
        def _(t, g=g):
            band = g * 16 + t
            if g == 0:
                value = planes[0, t]
            elif g == 4:
                value = planes[3, 16 + t]
            else:
                value = planes[g, t] + planes[g - 1, 16 + t]
            under = jnp.where(top, divisor[0, pl.ds(band, 1), :], divisor[1, pl.ds(band, 1), :])
            value = value / under
            turned = pltpu.roll(value, 4, 0)
            ready[2 * band] = jnp.where(top, value, turned)
            ready[2 * band + 1] = jnp.where(top, turned, value)

    def last_copy(d):
        peer = (e + d) % 32
        return remote(outgoing.at[peer], incoming.at[e], last_send.at[d], last_recv.at[d], {"exp": peer})

    @pl.loop(0, 32)
    def _(d):
        owner = (e + d) % 32
        for t in range(3):
            a = ready[sites[owner * 5 + 2 * t]]
            b = ready[sites[owner * 5 + min(2 * t + 1, 4)]]
            outgoing[owner, t] = jnp.where(top, a, b)

        @pl.when(d > 0)
        def _():
            last_copy(d).start()

    keep = pltpu.make_async_copy(outgoing.at[e], incoming.at[e], own_sem)
    keep.start()

    @pl.loop(1, 32)
    def _(d):
        last_copy(d).wait()

    keep.wait()

    for slot in range(5):
        upper = sites[e * 5 + slot] % 2 == 0
        for blk in range(16):
            parts = []
            for core in range(2):
                a = incoming[exp_index(blk % 4, blk // 4, core), slot // 2]
                b = incoming[exp_index(blk // 4, blk % 4, core), slot // 2]
                v = jnp.where(upper, a, b)
                if core != slot % 2:
                    v = pltpu.roll(v, 4, 0)
                parts.append(v)
            out[slot, :, 128 * blk : 128 * blk + 128] = jnp.where(top, parts[0], parts[1])


def per_device(images, psf_coef, phases, col_shift, band_offset, exposure_weight, patch_site):
    smem = pl.BlockSpec(memory_space=pltpu.SMEM)
    vmem = pl.BlockSpec(memory_space=pltpu.VMEM)
    dma = pltpu.SemaphoreType.DMA
    return pl.pallas_call(
        coadd_kernel,
        out_shape=jax.ShapeDtypeStruct((5, 8, 2048), F32),
        in_specs=[pl.BlockSpec(memory_space=pl.ANY)] + [smem] * 7,
        out_specs=vmem,
        scratch_shapes=[
            pltpu.VMEM((EXT, COLS), F32),
            pltpu.VMEM((EXT, COLS + 2 * PADC), BF),
            pltpu.VMEM((EXT, COLS + 2 * PADC), BF),
            pltpu.VMEM((3, 512, 256), BF),
            pltpu.VMEM((3, 512, 256), BF),
            pltpu.VMEM((4, 128, 160), BF),
            pltpu.VMEM((4, 128, 160), BF),
            pltpu.VMEM((32, 8, 128), I32),
            pltpu.SMEM((16, 8, 128), I32),
            pltpu.VMEM((2, 16, 16, 2, 16, 128), BF),
            pltpu.VMEM((2, 3, 4, 16, 2, 16, 128), BF),
            pltpu.VMEM((2, 4, 32, 2, 16, 128), BF),
            pltpu.VMEM((2, 3, 32, 2, 16, 128), BF),
            pltpu.VMEM((2, 2, 32, 16, 128), F32),
            pltpu.VMEM((2, 32, 16, 128), F32),
            pltpu.VMEM((4, 32, 8, 128), F32),
            pltpu.VMEM((4, 32, 8, 128), F32),
            pltpu.VMEM((2, 128, 128), F32),
            pltpu.VMEM((160, 8, 128), F32),
            pltpu.VMEM((32, 3, 8, 128), F32),
            pltpu.VMEM((32, 3, 8, 128), F32),
            dma((4,)), dma((2,)), dma((2,)), dma((7,)), dma((7,)), dma,
            dma((2, 3, 2)), dma((2, 3, 2)), dma((2, 3)), dma((2, 3)), dma, dma,
            dma((3,)), dma((3,)), dma((32,)), dma((32,)), dma,
        ],
        compiler_params=pltpu.CompilerParams(
            collective_id=0, has_side_effects=True, vmem_limit_bytes=60 << 20
        ),
        name="coadd",
    )(
        images, psf_coef, phases, jnp.asarray(lanczos_table().reshape(-1)),
        col_shift, band_offset, exposure_weight.astype(F32), patch_site,
    )


def solution(mesh):
    placed = (P("exp", "seg", None), P("exp", None, None), P("exp", None), P("exp"), P("exp"), P("exp"), P())
    return jax.shard_map(per_device, mesh=mesh, in_specs=placed, out_specs=P("exp", "seg", None), check_vma=False)
```

```python
import functools
import numpy as np
import jax
import jax.numpy as jnp
from jax import lax
from jax.experimental import pallas as pl
from jax.experimental.pallas import tpu as pltpu
from jax.sharding import PartitionSpec as P

MESH = pl.DeviceIdType.MESH
BF = jnp.bfloat16
F32 = jnp.float32
I32 = jnp.int32
TAPS = 21
SIGMAS = (1.0, 2.0, 3.5)
HALO = 16
ROWS = 512
COLS = 4096
EXT = ROWS + 2 * HALO


def basis_numbers():
    u = np.arange(TAPS, dtype=np.float64) - TAPS // 2
    out = []
    for s in SIGMAS:
        g = np.exp(-u * u / (2.0 * s * s))
        out.append(g / g.sum())
    return np.stack(out)


def lanczos_table():
    rows = []
    for p in range(16):
        u = np.arange(6, dtype=np.float64) - 2.0 - p / 16.0
        v = np.sinc(u) * np.sinc(u / 3.0)
        rows.append(v / v.sum())
    return np.stack(rows).astype(np.float32)


BASIS = basis_numbers()


def here():
    s = lax.axis_index("seg")
    e = lax.axis_index("exp")
    return s, e // 8, (e // 2) % 4, e % 2


def exp_index(z, y, c):
    return (z * 4 + y) * 2 + c


def banded(shape, distance, numbers):
    out = jnp.zeros(shape, F32)
    for t, number in enumerate(numbers):
        out = jnp.where(distance == t, number, out)
    return out


def split(v):
    high = v.astype(BF)
    return high, (v - high.astype(F32)).astype(BF)


def dot(a, b):
    return jnp.dot(a, b, preferred_element_type=F32)


def exact_dot(a, b):
    return jnp.dot(a, b, precision=lax.Precision.HIGHEST, preferred_element_type=F32)


def taps_of(coef, axis):
    return [
        coef[0, axis, 0] * F32(BASIS[0, t])
        + coef[0, axis, 1] * F32(BASIS[1, t])
        + coef[0, axis, 2] * F32(BASIS[2, t])
        for t in range(TAPS)
    ]


def build_columns(coef, table, phases, shift_ref, cols):
    shift = shift_ref[0]
    kc = taps_of(coef, 1)
    phase = phases[0, 1]
    lz = [table[phase * 6 + n] for n in range(6)]
    k = lax.broadcasted_iota(I32, (256, 256), 0)
    m = lax.broadcasted_iota(I32, (256, 256), 1)
    inner = banded((256, 256), k - m + 10, kc)
    m = lax.broadcasted_iota(I32, (256, 128), 0)
    j = lax.broadcasted_iota(I32, (256, 128), 1)
    outer = banded((256, 128), m - j - 62 + shift, lz)
    for variant in range(3):
        part = outer
        if variant == 0:
            part = jnp.where(m >= 64, outer, 0.0)
        if variant == 2:
            part = jnp.where(m < 192, outer, 0.0)
        high, low = split(exact_dot(inner, part))
        cols[variant, :, 0:128] = high
        cols[variant, :, 128:256] = low


def build_rows(s, coef, table, phases, rhi, rlo):
    kr = taps_of(coef, 0)
    phase = phases[0, 0]
    lz = [table[phase * 6 + n] for n in range(6)]
    o = lax.broadcasted_iota(I32, (128, 144), 0)
    m = lax.broadcasted_iota(I32, (128, 144), 1)
    row = (o // 32) * 32 + ((o // 4) % 4) * 8 + ((o // 16) % 2) * 4 + o % 4
    outer = banded((128, 144), m - 6 - row, lz)
    m = lax.broadcasted_iota(I32, (144, 160), 0)
    k = lax.broadcasted_iota(I32, (144, 160), 1)
    inner = banded((144, 160), k - m + 2, kr)
    for block in range(4):
        place = s * ROWS + 128 * block - 8 + m
        part = jnp.where((place >= 0) & (place < 4 * ROWS), inner, 0.0)
        high, low = split(exact_dot(outer, part))
        rhi[block] = high
        rlo[block] = low


ORDER = (2, 1, 3, 0)


def coadd_kernel(
    image, coef, phases, table, shift_ref, offset_ref, weight_ref, sites,
    out,
    xf, xhi, xlo, cols, rhi, rlo, mids, meta, metas, sent, first, kept, crossed, partial, second,
    quarters, planes, divisor, ready, outgoing, incoming,
    load_sem, halo_send, halo_recv, meta_send, meta_recv, meta_load,
    first_send, first_recv, cross_send, cross_recv, second_send, second_recv,
    x_send, x_recv, last_send, last_recv, own_sem,
):
    s, z, y, c = here()
    e = exp_index(z, y, c)
    chunks = 4
    rows_each = ROWS // chunks
    barrier = pltpu.get_barrier_semaphore()
    xpeers = {d: {"seg": (s + d) % 4} for d in (1, 2, 3)}
    ypeers = {d: {"exp": exp_index(z, (y + d) % 4, c)} for d in (1, 2, 3)}
    zpeers = {d: {"exp": exp_index((z + d) % 4, y, c)} for d in (1, 2, 3)}
    partner = {"exp": exp_index(z, y, 1 - c)}
    for d in (1, 2, 3):
        pl.semaphore_signal(barrier, inc=1, device_id=xpeers[d], device_id_type=MESH)

    loads = []
    for i in range(chunks):
        cp = pltpu.make_async_copy(
            image.at[0, pl.ds(i * rows_each, rows_each)],
            xf.at[pl.ds(HALO + i * rows_each, rows_each)],
            load_sem.at[i],
        )
        cp.start()
        loads.append(cp)

    @pl.loop(1, 32)
    def _(d):
        pl.semaphore_signal(barrier, inc=1, device_id={"exp": (e + d) % 32}, device_id_type=MESH)

    mine = c * 16 + z * 4 + y
    line = lax.broadcasted_iota(I32, (8, 128), 0)
    scaled = (weight_ref[0] * 256.0).astype(I32)
    meta[mine] = jnp.where(line == 0, offset_ref[0], jnp.where(line == 1, shift_ref[0], scaled))

    def remote(src, dst, send, recv, peer):
        return pltpu.make_async_remote_copy(
            src_ref=src, dst_ref=dst, send_sem=send, recv_sem=recv, device_id=peer, device_id_type=MESH
        )

    halos = [
        remote(image.at[0, pl.ds(ROWS - HALO, HALO)], xf.at[pl.ds(0, HALO)],
               halo_send.at[0], halo_recv.at[0], xpeers[1]),
        remote(image.at[0, pl.ds(0, HALO)], xf.at[pl.ds(HALO + ROWS, HALO)],
               halo_send.at[1], halo_recv.at[1], xpeers[3]),
    ]
    build_columns(coef, table, phases, shift_ref, cols)
    pl.semaphore_wait(barrier, 34)
    for cp in halos:
        cp.start()
    own = meta.at[mine]
    step = [remote(own, own, meta_send.at[d - 1], meta_recv.at[d - 1], ypeers[d]) for d in (1, 2, 3)]
    for cp in step:
        cp.start()
    build_rows(s, coef, table, phases, rhi, rlo)

    def convert(start, count, keep=None):
        rows = pl.ds(start, count)
        value = xf[rows, :]
        if keep is not None:
            value = jnp.where(keep, value, 0.0)
        edge = jnp.zeros((count, 64), F32)
        high, low = split(jnp.concatenate([edge, value, edge], axis=1))
        xhi[rows, :] = high
        xlo[rows, :] = low

    def convert_chunk(i):
        loads[i].wait()

        @pl.loop(0, rows_each // 16)
        def _(t):
            convert(pl.multiple_of(HALO + i * rows_each + t * 16, 16), 16)

    convert_chunk(0)
    convert_chunk(1)
    for cp in step:
        cp.wait()
    group = meta.at[pl.ds(c * 16 + z * 4, 4)]
    step = [remote(group, group, meta_send.at[2 + d], meta_recv.at[2 + d], zpeers[d]) for d in (1, 2, 3)]
    for cp in step:
        cp.start()
    convert_chunk(2)
    convert_chunk(3)

    weight = weight_ref[0]

    def across(h, jh, rows):
        parts = []
        for side in range(2):
            block = h * 16 + jh * 2 + side
            variant = jnp.where(block == 0, 0, jnp.where(block == 31, 2, 1))
            window = pl.ds(pl.multiple_of(block * 128, 128), 256)
            both = dot(xhi[rows, window], cols[variant])
            cross = dot(xlo[rows, window], cols[variant, :, 0:128])
            parts.append(both[:, 0:128] + both[:, 128:256] + cross)
        return split(jnp.concatenate(parts, axis=1))

    def down(h, jh, take):
        for block in range(4):
            a, b = take(slice(128 * block, 128 * block + 160))
            rh, rl = rhi[block], rlo[block]
            got = ((dot(rh, a) + dot(rl, a) + dot(rh, b)) * weight).astype(BF)
            for part in range(2):
                sent[h, jh * 2 + part, 4 * block : 4 * block + 4] = got[
                    :, 128 * part : 128 * part + 128
                ].reshape(4, 2, 16, 128)

    def first_copy(h, d, side, place):
        peers = (ypeers, zpeers)[h]
        return remote(
            sent.at[h, pl.ds(place, 2)], first.at[h, d - 1, pl.ds(side * 2, 2)],
            first_send.at[h, d - 1, side], first_recv.at[h, d - 1, side], peers[d],
        )

    def step_of(h, d, side):
        return (((y, z)[h] + d) % 4) * 2 + side

    inner_rows = slice(HALO, HALO + ROWS)

    @pl.loop(0, 2)
    def _(side):
        for h in range(2):
            high, low = across(h, step_of(h, ORDER[0], side), inner_rows)
            mids[side * 2 + h, 0, inner_rows, :] = high
            mids[side * 2 + h, 1, inner_rows, :] = low

    for cp in step:
        cp.wait()
    half = meta.at[pl.ds(c * 16, 16)]
    metas_copy = pltpu.make_async_copy(half, metas, meta_load)
    metas_copy.start()
    last_meta = remote(half, half, meta_send.at[6], meta_recv.at[6], partner)
    last_meta.start()
    for cp in halos:
        cp.wait()
    convert(0, HALO, s > 0)
    convert(HALO + ROWS, HALO, s < 3)

    @pl.loop(0, 2)
    def _(side):
        for h in range(2):
            jh = step_of(h, ORDER[0], side)
            slot = side * 2 + h
            for start in (0, HALO + ROWS):
                edge_rows = slice(start, start + HALO)
                high, low = across(h, jh, edge_rows)
                mids[slot, 0, edge_rows, :] = high
                mids[slot, 1, edge_rows, :] = low
            down(h, jh, lambda rows: (mids[slot, 0, rows, :], mids[slot, 1, rows, :]))
            first_copy(h, ORDER[0], side, jh * 2).start()

    for d in ORDER[1:]:

        @pl.loop(0, 2)
        def _(side, d=d):
            for h in range(2):
                jh = step_of(h, d, side)
                high, low = across(h, jh, slice(0, EXT))
                down(h, jh, lambda rows: (high[rows], low[rows]))
                if d:
                    first_copy(h, d, side, jh * 2).start()

    last_meta.wait()
    metas_copy.wait()

    off = meta[:, 0, :]
    shift = meta[:, 1, :]
    heavy = meta[:, 2, :].astype(F32) * (1.0 / 256.0)
    lane = lax.broadcasted_iota(I32, (32, 128), 1)
    inband = jnp.where((lane >= off) & (lane < off + 64), 1.0, 0.0).T
    for h in range(2):
        block = (4 * y + z, 4 * z + y)[h]
        col = h * 2048 + block * 128 + lane - shift
        cover = jnp.where((col >= 0) & (col < COLS), heavy, 0.0)
        divisor[h] = jnp.maximum(dot(inband.astype(BF), cover.astype(BF)), 1.0)

    for h in range(2):
        for d in (2, 1, 3):
            for side in range(2):
                first_copy(h, d, side, 0).wait()

    def block_of(h, d):
        return ((z, y)[h] + d) % 4

    def cross_copy(h, d):
        place = h * 4 + d
        return remote(crossed.at[0, h, d], crossed.at[1, h, d], cross_send.at[place], cross_recv.at[place], partner)

    def second_copy(h, d):
        peers = (zpeers, ypeers)[h]
        return remote(
            partial.at[h, d], second.at[h, d - 1], second_send.at[h, d - 1], second_recv.at[h, d - 1], peers[d]
        )

    def gather_block(h, d):
        block = block_of(h, d)
        starts = []
        for k in range(4):
            row = z * 4 + (y + 4 - k) % 4 if h == 0 else ((z + 4 - k) % 4) * 4 + y
            starts.append(metas[row, 0, 0])

        @pl.loop(0, 32, unroll=4)
        def _(band):
            acc = jnp.zeros((2, 16, 128), F32)
            for k in range(4):
                local = band - starts[k]
                valid = (local >= 0) & (local < 16)
                at = jnp.clip(local, 0, 15)
                if k == 0:
                    piece = sent[h, (y, z)[h] * 4 + block, at]
                else:
                    piece = first[h, k - 1, block, at]
                acc = acc + jnp.where(valid, piece, jnp.zeros_like(piece)).astype(F32)
            kept[h, d, band] = jnp.where(c == 0, acc[0], acc[1])
            crossed[0, h, d, band] = jnp.where(c == 0, acc[1], acc[0])

        cross_copy(h, d).start()

    def pass_block(h, d):
        cross_copy(h, d).wait()

        @pl.loop(0, 32, unroll=4)
        def _(band):
            partial[h, d, band] = (kept[h, d, band] + crossed[1, h, d, band]).astype(BF)

        if d:
            second_copy(h, d).start()

    todo = [(h, d) for d in ORDER for h in range(2)]
    for n in range(len(todo) + 2):
        if n < len(todo):
            gather_block(*todo[n])
        if n >= 2:
            pass_block(*todo[n - 2])

    for h in range(2):
        for d in (1, 2, 3):
            second_copy(h, d).wait()

    @pl.loop(0, 32, unroll=4)
    def _(band):
        sums = []
        for h in range(2):
            acc = partial[h, 0, band].astype(F32)
            for k in range(3):
                acc = acc + second[h, k, band].astype(F32)
            sums.append(acc)
        a, b = sums
        for q in range(4):
            quarters[q, band] = jnp.concatenate([a[4 * q : 4 * q + 4], b[4 * q : 4 * q + 4]], axis=0)

    moves = []
    for d in (2, 1, 3):
        cp = remote(quarters.at[(s + d) % 4], planes.at[s], x_send.at[d - 1], x_recv.at[d - 1], xpeers[d])
        cp.start()
        moves.append(cp)
    planes[s] = quarters[s]
    for cp in moves:
        cp.wait()

    top = line < 4
    for g in range(5):

        @pl.loop(0, 16, unroll=4)
        def _(t, g=g):
            band = g * 16 + t
            if g == 0:
                value = planes[0, t]
            elif g == 4:
                value = planes[3, 16 + t]
            else:
                value = planes[g, t] + planes[g - 1, 16 + t]
            under = jnp.where(top, divisor[0, pl.ds(band, 1), :], divisor[1, pl.ds(band, 1), :])
            value = value / under
            turned = pltpu.roll(value, 4, 0)
            ready[2 * band] = jnp.where(top, value, turned)
            ready[2 * band + 1] = jnp.where(top, turned, value)

    def last_copy(d):
        peer = (e + d) % 32
        return remote(outgoing.at[peer], incoming.at[e], last_send.at[d], last_recv.at[d], {"exp": peer})

    @pl.loop(0, 32)
    def _(d):
        owner = (e + d) % 32
        for t in range(3):
            a = ready[sites[owner * 5 + 2 * t]]
            b = ready[sites[owner * 5 + min(2 * t + 1, 4)]]
            outgoing[owner, t] = jnp.where(top, a, b)

        @pl.when(d > 0)
        def _():
            last_copy(d).start()

    keep = pltpu.make_async_copy(outgoing.at[e], incoming.at[e], own_sem)
    keep.start()

    @pl.loop(1, 32)
    def _(d):
        last_copy(d).wait()

    keep.wait()

    for slot in range(5):
        upper = sites[e * 5 + slot] % 2 == 0
        for blk in range(16):
            parts = []
            for core in range(2):
                a = incoming[exp_index(blk % 4, blk // 4, core), slot // 2]
                b = incoming[exp_index(blk // 4, blk % 4, core), slot // 2]
                v = jnp.where(upper, a, b)
                if core != slot % 2:
                    v = pltpu.roll(v, 4, 0)
                parts.append(v)
            out[slot, :, 128 * blk : 128 * blk + 128] = jnp.where(top, parts[0], parts[1])


def per_device(images, psf_coef, phases, col_shift, band_offset, exposure_weight, patch_site):
    smem = pl.BlockSpec(memory_space=pltpu.SMEM)
    vmem = pl.BlockSpec(memory_space=pltpu.VMEM)
    dma = pltpu.SemaphoreType.DMA
    return pl.pallas_call(
        coadd_kernel,
        out_shape=jax.ShapeDtypeStruct((5, 8, 2048), F32),
        in_specs=[pl.BlockSpec(memory_space=pl.ANY)] + [smem] * 7,
        out_specs=vmem,
        scratch_shapes=[
            pltpu.VMEM((EXT, COLS), F32),
            pltpu.VMEM((EXT, COLS + 128), BF),
            pltpu.VMEM((EXT, COLS + 128), BF),
            pltpu.VMEM((3, 256, 256), BF),
            pltpu.VMEM((4, 128, 160), BF),
            pltpu.VMEM((4, 128, 160), BF),
            pltpu.VMEM((4, 2, EXT, 256), BF),
            pltpu.VMEM((32, 8, 128), I32),
            pltpu.SMEM((16, 8, 128), I32),
            pltpu.VMEM((2, 16, 16, 2, 16, 128), BF),
            pltpu.VMEM((2, 3, 4, 16, 2, 16, 128), BF),
            pltpu.VMEM((2, 4, 32, 16, 128), F32),
            pltpu.VMEM((2, 2, 4, 32, 16, 128), F32),
            pltpu.VMEM((2, 4, 32, 16, 128), BF),
            pltpu.VMEM((2, 3, 32, 16, 128), BF),
            pltpu.VMEM((4, 32, 8, 128), F32),
            pltpu.VMEM((4, 32, 8, 128), F32),
            pltpu.VMEM((2, 128, 128), F32),
            pltpu.VMEM((160, 8, 128), F32),
            pltpu.VMEM((32, 3, 8, 128), F32),
            pltpu.VMEM((32, 3, 8, 128), F32),
            dma((4,)), dma((2,)), dma((2,)), dma((7,)), dma((7,)), dma,
            dma((2, 3, 2)), dma((2, 3, 2)), dma((8,)), dma((8,)), dma((2, 3)), dma((2, 3)),
            dma((3,)), dma((3,)), dma((32,)), dma((32,)), dma,
        ],
        compiler_params=pltpu.CompilerParams(
            collective_id=0, has_side_effects=True, vmem_limit_bytes=60 << 20
        ),
        name="coadd",
    )(
        images, psf_coef, phases, jnp.asarray(lanczos_table().reshape(-1)),
        col_shift, band_offset, exposure_weight.astype(F32), patch_site,
    )


def solution(mesh):
    placed = (P("exp", "seg", None), P("exp", None, None), P("exp", None), P("exp"), P("exp"), P("exp"), P())
    return jax.shard_map(per_device, mesh=mesh, in_specs=placed, out_specs=P("exp", "seg", None), check_vma=False)
```

```python
import functools
import numpy as np
import jax
import jax.numpy as jnp
from jax import lax
from jax.experimental import pallas as pl
from jax.experimental.pallas import tpu as pltpu
from jax.sharding import PartitionSpec as P

MESH = pl.DeviceIdType.MESH
BF = jnp.bfloat16
F32 = jnp.float32
I32 = jnp.int32
TAPS = 21
SIGMAS = (1.0, 2.0, 3.5)
HALO = 16
ROWS = 512
COLS = 4096
EXT = ROWS + 2 * HALO


def basis_numbers():
    u = np.arange(TAPS, dtype=np.float64) - TAPS // 2
    out = []
    for s in SIGMAS:
        g = np.exp(-u * u / (2.0 * s * s))
        out.append(g / g.sum())
    return np.stack(out)


def lanczos_table():
    rows = []
    for p in range(16):
        u = np.arange(6, dtype=np.float64) - 2.0 - p / 16.0
        v = np.sinc(u) * np.sinc(u / 3.0)
        rows.append(v / v.sum())
    return np.stack(rows).astype(np.float32)


BASIS = basis_numbers()


def here():
    s = lax.axis_index("seg")
    e = lax.axis_index("exp")
    return s, e // 8, (e // 2) % 4, e % 2


def exp_index(z, y, c):
    return (z * 4 + y) * 2 + c


def banded(shape, distance, numbers):
    out = jnp.zeros(shape, F32)
    for t, number in enumerate(numbers):
        out = jnp.where(distance == t, number, out)
    return out


def split(v):
    high = v.astype(BF)
    return high, (v - high.astype(F32)).astype(BF)


def dot(a, b):
    return jnp.dot(a, b, preferred_element_type=F32)


def exact_dot(a, b):
    return jnp.dot(a, b, precision=lax.Precision.HIGHEST, preferred_element_type=F32)


def taps_of(coef, axis):
    return [
        coef[0, axis, 0] * F32(BASIS[0, t])
        + coef[0, axis, 1] * F32(BASIS[1, t])
        + coef[0, axis, 2] * F32(BASIS[2, t])
        for t in range(TAPS)
    ]


def build_columns(coef, table, phases, shift_ref, cols):
    shift = shift_ref[0]
    kc = taps_of(coef, 1)
    phase = phases[0, 1]
    lz = [table[phase * 6 + n] for n in range(6)]
    k = lax.broadcasted_iota(I32, (256, 256), 0)
    m = lax.broadcasted_iota(I32, (256, 256), 1)
    inner = banded((256, 256), k - m + 10, kc)
    m = lax.broadcasted_iota(I32, (256, 128), 0)
    j = lax.broadcasted_iota(I32, (256, 128), 1)
    outer = banded((256, 128), m - j - 62 + shift, lz)
    for variant in range(3):
        part = outer
        if variant == 0:
            part = jnp.where(m >= 64, outer, 0.0)
        if variant == 2:
            part = jnp.where(m < 192, outer, 0.0)
        high, low = split(exact_dot(inner, part))
        cols[variant, :, 0:128] = high
        cols[variant, :, 128:256] = low


def build_rows(s, coef, table, phases, rhi, rlo):
    kr = taps_of(coef, 0)
    phase = phases[0, 0]
    lz = [table[phase * 6 + n] for n in range(6)]
    o = lax.broadcasted_iota(I32, (128, 144), 0)
    m = lax.broadcasted_iota(I32, (128, 144), 1)
    row = (o // 32) * 32 + ((o // 4) % 4) * 8 + ((o // 16) % 2) * 4 + o % 4
    outer = banded((128, 144), m - 6 - row, lz)
    m = lax.broadcasted_iota(I32, (144, 160), 0)
    k = lax.broadcasted_iota(I32, (144, 160), 1)
    inner = banded((144, 160), k - m + 2, kr)
    for block in range(4):
        place = s * ROWS + 128 * block - 8 + m
        part = jnp.where((place >= 0) & (place < 4 * ROWS), inner, 0.0)
        high, low = split(exact_dot(outer, part))
        rhi[block] = high
        rlo[block] = low


ORDER = (2, 1, 3, 0)


def coadd_kernel(
    image, coef, phases, table, shift_ref, offset_ref, weight_ref, sites,
    out,
    xf, xhi, xlo, cols, rhi, rlo, mids, meta, metas, sent, first, kept, crossed, partial, second,
    quarters, planes, divisor, ready, outgoing, incoming,
    load_sem, halo_send, halo_recv, meta_send, meta_recv, meta_load,
    first_send, first_recv, cross_send, cross_recv, second_send, second_recv,
    x_send, x_recv, last_send, last_recv, own_sem,
):
    s, z, y, c = here()
    e = exp_index(z, y, c)
    chunks = 4
    rows_each = ROWS // chunks
    barrier = pltpu.get_barrier_semaphore()
    xpeers = {d: {"seg": (s + d) % 4} for d in (1, 2, 3)}
    ypeers = {d: {"exp": exp_index(z, (y + d) % 4, c)} for d in (1, 2, 3)}
    zpeers = {d: {"exp": exp_index((z + d) % 4, y, c)} for d in (1, 2, 3)}
    partner = {"exp": exp_index(z, y, 1 - c)}
    near = [peers[d] for peers in (xpeers, ypeers, zpeers) for d in (1, 3, 2)] + [partner]
    for peer in near:
        pl.semaphore_signal(barrier, inc=1, device_id=peer, device_id_type=MESH)

    loads = []
    for i in range(chunks):
        cp = pltpu.make_async_copy(
            image.at[0, pl.ds(i * rows_each, rows_each)],
            xf.at[pl.ds(HALO + i * rows_each, rows_each)],
            load_sem.at[i],
        )
        cp.start()
        loads.append(cp)

    mine = c * 16 + z * 4 + y
    line = lax.broadcasted_iota(I32, (8, 128), 0)
    scaled = (weight_ref[0] * 256.0).astype(I32)
    meta[mine] = jnp.where(line == 0, offset_ref[0], jnp.where(line == 1, shift_ref[0], scaled))

    def remote(src, dst, send, recv, peer):
        return pltpu.make_async_remote_copy(
            src_ref=src, dst_ref=dst, send_sem=send, recv_sem=recv, device_id=peer, device_id_type=MESH
        )

    halos = [
        remote(image.at[0, pl.ds(ROWS - HALO, HALO)], xf.at[pl.ds(0, HALO)],
               halo_send.at[0], halo_recv.at[0], xpeers[1]),
        remote(image.at[0, pl.ds(0, HALO)], xf.at[pl.ds(HALO + ROWS, HALO)],
               halo_send.at[1], halo_recv.at[1], xpeers[3]),
    ]
    build_columns(coef, table, phases, shift_ref, cols)
    pl.semaphore_wait(barrier, len(near))
    for cp in halos:
        cp.start()
    own = meta.at[mine]
    step = [remote(own, own, meta_send.at[d - 1], meta_recv.at[d - 1], ypeers[d]) for d in (1, 2, 3)]
    for cp in step:
        cp.start()
    build_rows(s, coef, table, phases, rhi, rlo)

    def convert(source, target, count, keep=None):
        value = xf[pl.ds(source, count), :]
        if keep is not None:
            value = jnp.where(keep, value, 0.0)
        edge = jnp.zeros((count, 64), F32)
        high, low = split(jnp.concatenate([edge, value, edge], axis=1))
        xhi[pl.ds(target, count), :] = high
        xlo[pl.ds(target, count), :] = low

    def convert_chunk(i):
        loads[i].wait()

        @pl.loop(0, rows_each // 16)
        def _(t):
            start = pl.multiple_of(i * rows_each + t * 16, 16)
            convert(HALO + start, start, 16)

    convert_chunk(0)
    convert_chunk(1)
    for cp in step:
        cp.wait()
    group = meta.at[pl.ds(c * 16 + z * 4, 4)]
    step = [remote(group, group, meta_send.at[2 + d], meta_recv.at[2 + d], zpeers[d]) for d in (1, 2, 3)]
    for cp in step:
        cp.start()
    convert_chunk(2)
    convert_chunk(3)

    weight = weight_ref[0]

    def across(h, jh, rows):
        parts = []
        for side in range(2):
            block = h * 16 + jh * 2 + side
            variant = jnp.where(block == 0, 0, jnp.where(block == 31, 2, 1))
            window = pl.ds(pl.multiple_of(block * 128, 128), 256)
            both = dot(xhi[rows, window], cols[variant])
            cross = dot(xlo[rows, window], cols[variant, :, 0:128])
            parts.append(both[:, 0:128] + both[:, 128:256] + cross)
        return split(jnp.concatenate(parts, axis=1))

    def own_rows(h, jh, slot):
        high, low = across(h, jh, slice(0, ROWS))
        mids[slot, 0, HALO : HALO + ROWS, :] = high
        mids[slot, 1, HALO : HALO + ROWS, :] = low

    def edge_rows(h, jh, slot):
        for half, value in enumerate(across(h, jh, slice(ROWS, EXT))):
            mids[slot, half, 0:HALO, :] = value[0:HALO]
            mids[slot, half, HALO + ROWS : EXT, :] = value[HALO : 2 * HALO]

    def down(h, jh, slot, blocks):
        for block in blocks:
            rows = slice(128 * block, 128 * block + 160)
            a, b = mids[slot, 0, rows, :], mids[slot, 1, rows, :]
            rh, rl = rhi[block], rlo[block]
            got = ((dot(rh, a) + dot(rl, a) + dot(rh, b)) * weight).astype(BF)
            for part in range(2):
                sent[h, jh * 2 + part, 4 * block : 4 * block + 4] = got[
                    :, 128 * part : 128 * part + 128
                ].reshape(4, 2, 16, 128)

    PIECES = ((4, 8), (0, 4), (12, 4))

    def first_copy(h, d, side, place, piece):
        peers = (ypeers, zpeers)[h]
        bands = pl.ds(*PIECES[piece])
        return remote(
            sent.at[h, pl.ds(place, 2), bands], first.at[h, d - 1, pl.ds(side * 2, 2), bands],
            first_send.at[h, d - 1, side, piece], first_recv.at[h, d - 1, side, piece], peers[d],
        )

    def step_of(h, d, side):
        return (((y, z)[h] + d) % 4) * 2 + side

    for d in (2, 1, 3):

        @pl.loop(0, 2)
        def _(side, d=d):
            for h in range(2):
                jh = step_of(h, d, side)
                slot = h * 8 + jh
                own_rows(h, jh, slot)
                down(h, jh, slot, (1, 2))
                first_copy(h, d, side, jh * 2, 0).start()

    for cp in step:
        cp.wait()
    half = meta.at[pl.ds(c * 16, 16)]
    metas_copy = pltpu.make_async_copy(half, metas, meta_load)
    metas_copy.start()
    last_meta = remote(half, half, meta_send.at[6], meta_recv.at[6], partner)
    last_meta.start()
    for cp in halos:
        cp.wait()
    convert(0, ROWS, HALO, s > 0)
    convert(HALO + ROWS, ROWS + HALO, HALO, s < 3)

    for d in (2, 1, 3):

        @pl.loop(0, 2)
        def _(side, d=d):
            for h in range(2):
                jh = step_of(h, d, side)
                slot = h * 8 + jh
                edge_rows(h, jh, slot)
                down(h, jh, slot, (0, 3))
                first_copy(h, d, side, jh * 2, 1).start()
                first_copy(h, d, side, jh * 2, 2).start()

    @pl.loop(0, 2)
    def _(side):
        for h in range(2):
            jh = step_of(h, 0, side)
            slot = h * 8 + jh
            own_rows(h, jh, slot)
            edge_rows(h, jh, slot)
            down(h, jh, slot, range(4))

    last_meta.wait()
    metas_copy.wait()

    off = meta[:, 0, :]
    shift = meta[:, 1, :]
    heavy = meta[:, 2, :].astype(F32) * (1.0 / 256.0)
    lane = lax.broadcasted_iota(I32, (32, 128), 1)
    inband = jnp.where((lane >= off) & (lane < off + 64), 1.0, 0.0).T
    for h in range(2):
        block = (4 * y + z, 4 * z + y)[h]
        col = h * 2048 + block * 128 + lane - shift
        cover = jnp.where((col >= 0) & (col < COLS), heavy, 0.0)
        divisor[h] = jnp.maximum(dot(inband.astype(BF), cover.astype(BF)), 1.0)

    for h in range(2):
        for d in (2, 1, 3):
            for side in range(2):
                for piece in range(3):
                    first_copy(h, d, side, 0, piece).wait()

    def block_of(h, d):
        return ((z, y)[h] + d) % 4

    def cross_copy(h, d):
        place = h * 4 + d
        return remote(crossed.at[0, h, d], crossed.at[1, h, d], cross_send.at[place], cross_recv.at[place], partner)

    def second_copy(h, d):
        peers = (zpeers, ypeers)[h]
        return remote(
            partial.at[h, d], second.at[h, d - 1], second_send.at[h, d - 1], second_recv.at[h, d - 1], peers[d]
        )

    def gather_block(h, d):
        block = block_of(h, d)
        starts = []
        for k in range(4):
            row = z * 4 + (y + 4 - k) % 4 if h == 0 else ((z + 4 - k) % 4) * 4 + y
            starts.append(metas[row, 0, 0])

        @pl.loop(0, 32, unroll=4)
        def _(band):
            acc = jnp.zeros((2, 16, 128), F32)
            for k in range(4):
                local = band - starts[k]
                valid = (local >= 0) & (local < 16)
                at = jnp.clip(local, 0, 15)
                if k == 0:
                    piece = sent[h, (y, z)[h] * 4 + block, at]
                else:
                    piece = first[h, k - 1, block, at]
                acc = acc + jnp.where(valid, piece, jnp.zeros_like(piece)).astype(F32)
            kept[h, d, band] = jnp.where(c == 0, acc[0], acc[1])
            crossed[0, h, d, band] = jnp.where(c == 0, acc[1], acc[0])

        cross_copy(h, d).start()

    def pass_block(h, d):
        cross_copy(h, d).wait()

        @pl.loop(0, 32, unroll=4)
        def _(band):
            partial[h, d, band] = (kept[h, d, band] + crossed[1, h, d, band]).astype(BF)

        if d:
            second_copy(h, d).start()

    todo = [(h, d) for d in ORDER for h in range(2)]
    for n in range(len(todo) + 2):
        if n < len(todo):
            gather_block(*todo[n])
        if n >= 2:
            pass_block(*todo[n - 2])

    for h in range(2):
        for d in (1, 2, 3):
            second_copy(h, d).wait()

    @pl.loop(0, 16, unroll=2)
    def _(pair):
        lines = [[] for _ in range(4)]
        for odd in range(2):
            band = 2 * pair + odd
            for h in range(2):
                acc = partial[h, 0, band].astype(F32)
                for k in range(3):
                    acc = acc + second[h, k, band].astype(F32)
                for q in range(4):
                    lines[q].append(acc[4 * q : 4 * q + 4])
        for q in range(4):
            quarters[q, pair] = jnp.concatenate(lines[q], axis=0).astype(BF)

    moves = []
    for d in (2, 1, 3):
        cp = remote(quarters.at[(s + d) % 4], planes.at[s], x_send.at[d - 1], x_recv.at[d - 1], xpeers[d])
        cp.start()
        moves.append(cp)
    planes[s] = quarters[s]
    for cp in moves:
        cp.wait()

    top = line < 4
    for g in range(5):

        @pl.loop(0, 8, unroll=2)
        def _(pair, g=g):
            if g == 0:
                both = planes[0, pair].astype(F32)
            elif g == 4:
                both = planes[3, 8 + pair].astype(F32)
            else:
                both = planes[g, pair].astype(F32) + planes[g - 1, 8 + pair].astype(F32)
            for odd in range(2):
                band = g * 16 + 2 * pair + odd
                under = jnp.where(top, divisor[0, pl.ds(band, 1), :], divisor[1, pl.ds(band, 1), :])
                value = both[8 * odd : 8 * odd + 8] / under
                turned = pltpu.roll(value, 4, 0)
                ready[2 * band] = jnp.where(top, value, turned)
                ready[2 * band + 1] = jnp.where(top, turned, value)

    def last_copy(d):
        peer = (e + d) % 32
        return remote(outgoing.at[peer], incoming.at[e], last_send.at[d], last_recv.at[d], {"exp": peer})

    @pl.loop(0, 32)
    def _(d):
        owner = (e + d) % 32
        for t in range(3):
            a = ready[sites[owner * 5 + 2 * t]]
            b = ready[sites[owner * 5 + min(2 * t + 1, 4)]]
            outgoing[owner, t] = jnp.where(top, a, b)

        @pl.when(d > 0)
        def _():
            last_copy(d).start()

    keep = pltpu.make_async_copy(outgoing.at[e], incoming.at[e], own_sem)
    keep.start()

    @pl.loop(1, 32)
    def _(d):
        last_copy(d).wait()

    keep.wait()

    for slot in range(5):
        upper = sites[e * 5 + slot] % 2 == 0
        for blk in range(16):
            parts = []
            for core in range(2):
                a = incoming[exp_index(blk % 4, blk // 4, core), slot // 2]
                b = incoming[exp_index(blk // 4, blk % 4, core), slot // 2]
                v = jnp.where(upper, a, b)
                if core != slot % 2:
                    v = pltpu.roll(v, 4, 0)
                parts.append(v)
            out[slot, :, 128 * blk : 128 * blk + 128] = jnp.where(top, parts[0], parts[1])


def per_device(images, psf_coef, phases, col_shift, band_offset, exposure_weight, patch_site):
    smem = pl.BlockSpec(memory_space=pltpu.SMEM)
    vmem = pl.BlockSpec(memory_space=pltpu.VMEM)
    dma = pltpu.SemaphoreType.DMA
    return pl.pallas_call(
        coadd_kernel,
        out_shape=jax.ShapeDtypeStruct((5, 8, 2048), F32),
        in_specs=[pl.BlockSpec(memory_space=pl.ANY)] + [smem] * 7,
        out_specs=vmem,
        scratch_shapes=[
            pltpu.VMEM((EXT, COLS), F32),
            pltpu.VMEM((EXT, COLS + 128), BF),
            pltpu.VMEM((EXT, COLS + 128), BF),
            pltpu.VMEM((3, 256, 256), BF),
            pltpu.VMEM((4, 128, 160), BF),
            pltpu.VMEM((4, 128, 160), BF),
            pltpu.VMEM((16, 2, EXT, 256), BF),
            pltpu.VMEM((32, 8, 128), I32),
            pltpu.SMEM((16, 8, 128), I32),
            pltpu.VMEM((2, 16, 16, 2, 16, 128), BF),
            pltpu.VMEM((2, 3, 4, 16, 2, 16, 128), BF),
            pltpu.VMEM((2, 4, 32, 16, 128), F32),
            pltpu.VMEM((2, 2, 4, 32, 16, 128), F32),
            pltpu.VMEM((2, 4, 32, 16, 128), BF),
            pltpu.VMEM((2, 3, 32, 16, 128), BF),
            pltpu.VMEM((4, 16, 16, 128), BF),
            pltpu.VMEM((4, 16, 16, 128), BF),
            pltpu.VMEM((2, 128, 128), F32),
            pltpu.VMEM((160, 8, 128), F32),
            pltpu.VMEM((32, 3, 8, 128), F32),
            pltpu.VMEM((32, 3, 8, 128), F32),
            dma((4,)), dma((2,)), dma((2,)), dma((7,)), dma((7,)), dma,
            dma((2, 3, 2, 3)), dma((2, 3, 2, 3)), dma((8,)), dma((8,)), dma((2, 3)), dma((2, 3)),
            dma((3,)), dma((3,)), dma((32,)), dma((32,)), dma,
        ],
        compiler_params=pltpu.CompilerParams(
            collective_id=0, has_side_effects=True, vmem_limit_bytes=60 << 20
        ),
        name="coadd",
    )(
        images, psf_coef, phases, jnp.asarray(lanczos_table().reshape(-1)),
        col_shift, band_offset, exposure_weight.astype(F32), patch_site,
    )


def solution(mesh):
    placed = (P("exp", "seg", None), P("exp", None, None), P("exp", None), P("exp"), P("exp"), P("exp"), P())
    return jax.shard_map(per_device, mesh=mesh, in_specs=placed, out_specs=P("exp", "seg", None), check_vma=False)
```

```python
import functools
import numpy as np
import jax
import jax.numpy as jnp
from jax import lax
from jax.experimental import pallas as pl
from jax.experimental.pallas import tpu as pltpu
from jax.sharding import PartitionSpec as P

MESH = pl.DeviceIdType.MESH
BF = jnp.bfloat16
F32 = jnp.float32
I32 = jnp.int32
TAPS = 21
SIGMAS = (1.0, 2.0, 3.5)
HALO = 16
ROWS = 512
COLS = 4096
EXT = ROWS + 2 * HALO


def basis_numbers():
    u = np.arange(TAPS, dtype=np.float64) - TAPS // 2
    out = []
    for s in SIGMAS:
        g = np.exp(-u * u / (2.0 * s * s))
        out.append(g / g.sum())
    return np.stack(out)


def lanczos_table():
    rows = []
    for p in range(16):
        u = np.arange(6, dtype=np.float64) - 2.0 - p / 16.0
        v = np.sinc(u) * np.sinc(u / 3.0)
        rows.append(v / v.sum())
    return np.stack(rows).astype(np.float32)


BASIS = basis_numbers()


def here():
    s = lax.axis_index("seg")
    e = lax.axis_index("exp")
    return s, e // 8, (e // 2) % 4, e % 2


def exp_index(z, y, c):
    return (z * 4 + y) * 2 + c


def banded(shape, distance, numbers):
    out = jnp.zeros(shape, F32)
    for t, number in enumerate(numbers):
        out = jnp.where(distance == t, number, out)
    return out


def split(v):
    high = v.astype(BF)
    return high, (v - high.astype(F32)).astype(BF)


def dot(a, b):
    return jnp.dot(a, b, preferred_element_type=F32)


def exact_dot(a, b):
    return jnp.dot(a, b, precision=lax.Precision.HIGHEST, preferred_element_type=F32)


def taps_of(coef, axis):
    return [
        coef[0, axis, 0] * F32(BASIS[0, t])
        + coef[0, axis, 1] * F32(BASIS[1, t])
        + coef[0, axis, 2] * F32(BASIS[2, t])
        for t in range(TAPS)
    ]


def build_columns(coef, table, phases, shift_ref, cols):
    shift = shift_ref[0]
    kc = taps_of(coef, 1)
    phase = phases[0, 1]
    lz = [table[phase * 6 + n] for n in range(6)]
    k = lax.broadcasted_iota(I32, (256, 256), 0)
    m = lax.broadcasted_iota(I32, (256, 256), 1)
    inner = banded((256, 256), k - m + 10, kc)
    apart = jnp.where((k < 128) == (m < 128), inner, 0.0)
    m = lax.broadcasted_iota(I32, (256, 128), 0)
    j = lax.broadcasted_iota(I32, (256, 128), 1)
    outer = banded((256, 128), m - j - 62 + shift, lz)
    seam = jnp.where((m < 128) == (j < 64), outer, 0.0)
    for variant, (left, right) in enumerate(((inner, outer), (apart, seam))):
        high, low = split(exact_dot(left, right))
        cols[variant, :, 0:128] = high
        cols[variant, :, 128:256] = low


def build_rows(s, coef, table, phases, rhi, rlo, blocks):
    kr = taps_of(coef, 0)
    phase = phases[0, 0]
    lz = [table[phase * 6 + n] for n in range(6)]
    o = lax.broadcasted_iota(I32, (128, 144), 0)
    m = lax.broadcasted_iota(I32, (128, 144), 1)
    row = (o // 32) * 32 + ((o // 4) % 4) * 8 + ((o // 16) % 2) * 4 + o % 4
    outer = banded((128, 144), m - 6 - row, lz)
    m = lax.broadcasted_iota(I32, (144, 160), 0)
    k = lax.broadcasted_iota(I32, (144, 160), 1)
    inner = banded((144, 160), k - m + 2, kr)
    for block in blocks:
        place = s * ROWS + 128 * block - 8 + m
        part = inner if block == 1 else jnp.where((place >= 0) & (place < 4 * ROWS), inner, 0.0)
        high, low = split(exact_dot(outer, part))
        rhi[block] = high
        rlo[block] = low


ORDER = (2, 1, 3, 0)


def coadd_kernel(
    image, coef, phases, table, shift_ref, offset_ref, weight_ref, sites,
    out,
    xf, cols, rhi, rlo, mids, meta, metas, sent, first_1, first_2, first_3, kept, early, leaving, arrived, partial, second,
    quarters, planes, divisor, ready, outgoing, incoming,
    load_sem, halo_send, halo_recv, meta_send, meta_recv, meta_load,
    first_send, first_recv, cross_send, cross_recv, second_send, second_recv,
    x_send, x_recv, last_send, last_recv, own_sem,
):
    s, z, y, c = here()
    e = exp_index(z, y, c)
    chunks = 4
    rows_each = ROWS // chunks
    barrier = pltpu.get_barrier_semaphore()
    xpeers = {d: {"seg": (s + d) % 4} for d in (1, 2, 3)}
    ypeers = {d: {"exp": exp_index(z, (y + d) % 4, c)} for d in (1, 2, 3)}
    zpeers = {d: {"exp": exp_index((z + d) % 4, y, c)} for d in (1, 2, 3)}
    partner = {"exp": exp_index(z, y, 1 - c)}
    near = [peers[d] for peers in (xpeers, ypeers, zpeers) for d in (1, 3, 2)] + [partner]
    for peer in near:
        pl.semaphore_signal(barrier, inc=1, device_id=peer, device_id_type=MESH)

    loads = []
    for i in range(chunks):
        cp = pltpu.make_async_copy(
            image.at[0, pl.ds(i * rows_each, rows_each)],
            xf.at[pl.ds(HALO + i * rows_each, rows_each)],
            load_sem.at[i],
        )
        cp.start()
        loads.append(cp)

    mine = c * 16 + z * 4 + y
    line = lax.broadcasted_iota(I32, (8, 128), 0)
    scaled = (weight_ref[0] * 256.0).astype(I32)
    meta[mine] = jnp.where(line == 0, offset_ref[0], jnp.where(line == 1, shift_ref[0], scaled))

    def remote(src, dst, send, recv, peer):
        return pltpu.make_async_remote_copy(
            src_ref=src, dst_ref=dst, send_sem=send, recv_sem=recv, device_id=peer, device_id_type=MESH
        )

    halos = [
        remote(image.at[0, pl.ds(ROWS - HALO, HALO)], xf.at[pl.ds(0, HALO)],
               halo_send.at[0], halo_recv.at[0], xpeers[1]),
        remote(image.at[0, pl.ds(0, HALO)], xf.at[pl.ds(HALO + ROWS, HALO)],
               halo_send.at[1], halo_recv.at[1], xpeers[3]),
    ]
    build_columns(coef, table, phases, shift_ref, cols)
    pl.semaphore_wait(barrier, len(near))
    for cp in halos:
        cp.start()
    own = meta.at[mine]
    step = [remote(own, own, meta_send.at[d - 1], meta_recv.at[d - 1], ypeers[d]) for d in (1, 2, 3)]
    for cp in step:
        cp.start()
    build_rows(s, coef, table, phases, rhi, rlo, (1,))

    for cp in loads:
        cp.wait()
    weight = weight_ref[0]

    def across(h, jh, fetch):
        first_tile = h * 16 + jh * 2
        high, low = [], []
        for k in range(3):
            tile = (first_tile + k) % 32
            a, b = split(fetch(pl.ds(pl.multiple_of(tile * 128, 128), 128)))
            high.append(a)
            low.append(b)
        parts = []
        for side in range(2):
            variant = jnp.where(first_tile + side == 31, 1, 0)
            a = jnp.concatenate(high[side : side + 2], axis=1)
            b = jnp.concatenate(low[side : side + 2], axis=1)
            both = dot(a, cols[variant])
            cross = dot(b, cols[variant, :, 0:128])
            parts.append(both[:, 0:128] + both[:, 128:256] + cross)
        return split(jnp.concatenate(parts, axis=1))

    def own_rows(h, jh, slot):
        high, low = across(h, jh, lambda tile: xf[HALO : HALO + ROWS, tile])
        mids[slot, 0, HALO : HALO + ROWS, :] = high
        mids[slot, 1, HALO : HALO + ROWS, :] = low

    def edge_fetch(tile):
        above = jnp.where(s > 0, xf[0:HALO, tile], 0.0)
        below = jnp.where(s < 3, xf[HALO + ROWS : EXT, tile], 0.0)
        return jnp.concatenate([above, below], axis=0)

    def edge_rows(h, jh, slot):
        for half, value in enumerate(across(h, jh, edge_fetch)):
            mids[slot, half, 0:HALO, :] = value[0:HALO]
            mids[slot, half, HALO + ROWS : EXT, :] = value[HALO : 2 * HALO]

    def down(h, jh, slot, blocks):
        for block in blocks:
            rows = slice(128 * block, 128 * block + 160)
            a, b = mids[slot, 0, rows, :], mids[slot, 1, rows, :]
            kind = 1 if block in (1, 2) else block
            rh, rl = rhi[kind], rlo[kind]
            got = ((dot(rh, a) + dot(rl, a) + dot(rh, b)) * weight).astype(BF)
            for part in range(2):
                sent[h, jh * 2 + part, 4 * block : 4 * block + 4] = got[
                    :, 128 * part : 128 * part + 128
                ].reshape(4, 2, 16, 128)

    first = {1: first_1, 2: first_2, 3: first_3}
    PIECES = ((4, 8), (0, 4), (12, 4))

    def first_copy(h, d, side, place, piece):
        peers = (ypeers, zpeers)[h]
        bands = pl.ds(*PIECES[piece])
        return remote(
            sent.at[h, pl.ds(place, 2), bands], first[d].at[h, pl.ds(side * 2, 2), bands],
            first_send.at[h, d - 1, side, piece], first_recv.at[h, d - 1, side, piece], peers[d],
        )

    def step_of(h, d, side):
        return (((y, z)[h] + d) % 4) * 2 + side

    for d in (2, 1, 3):

        @pl.loop(0, 2)
        def _(side, d=d):
            for h in range(2):
                jh = step_of(h, d, side)
                slot = h * 8 + jh
                own_rows(h, jh, slot)
                down(h, jh, slot, (1, 2))
                first_copy(h, d, side, jh * 2, 0).start()

    for cp in step:
        cp.wait()
    group = meta.at[pl.ds(c * 16 + z * 4, 4)]
    step = [remote(group, group, meta_send.at[2 + d], meta_recv.at[2 + d], zpeers[d]) for d in (1, 2, 3)]
    for cp in step:
        cp.start()
    build_rows(s, coef, table, phases, rhi, rlo, (0, 3))
    for cp in halos:
        cp.wait()

    for d in (2, 1, 3):

        @pl.loop(0, 2)
        def _(side, d=d):
            for h in range(2):
                jh = step_of(h, d, side)
                slot = h * 8 + jh
                edge_rows(h, jh, slot)
                down(h, jh, slot, (0, 3))
                first_copy(h, d, side, jh * 2, 1).start()
                first_copy(h, d, side, jh * 2, 2).start()

    for cp in step:
        cp.wait()
    half = meta.at[pl.ds(c * 16, 16)]
    metas_copy = pltpu.make_async_copy(half, metas, meta_load)
    metas_copy.start()
    last_meta = remote(half, half, meta_send.at[6], meta_recv.at[6], partner)
    last_meta.start()

    @pl.loop(0, 2)
    def _(side):
        for h in range(2):
            jh = step_of(h, 0, side)
            slot = h * 8 + jh
            own_rows(h, jh, slot)
            edge_rows(h, jh, slot)
            down(h, jh, slot, range(4))

    last_meta.wait()
    metas_copy.wait()

    off = meta[:, 0, :]
    shift = meta[:, 1, :]
    heavy = meta[:, 2, :].astype(F32) * (1.0 / 256.0)
    lane = lax.broadcasted_iota(I32, (32, 128), 1)
    inband = jnp.where((lane >= off) & (lane < off + 64), 1.0, 0.0).T
    for h in range(2):
        block = (4 * y + z, 4 * z + y)[h]
        col = (h * 2048 + block * 128 + 64 + lane) % COLS - shift
        cover = jnp.where((col >= 0) & (col < COLS), heavy, 0.0)
        divisor[h] = jnp.maximum(dot(inband.astype(BF), cover.astype(BF)), 1.0)

    def first_wait(d):
        for h in range(2):
            for side in range(2):
                for piece in range(3):
                    first_copy(h, d, side, 0, piece).wait()

    def block_of(h, d):
        return ((z, y)[h] + d) % 4

    def cross_copy(h, d):
        place = h * 4 + d
        return remote(leaving.at[h, d], arrived.at[h, d], cross_send.at[place], cross_recv.at[place], partner)

    def second_copy(h, d):
        peers = (zpeers, ypeers)[h]
        return remote(
            partial.at[h, d], second.at[h, d - 1], second_send.at[h, d - 1], second_recv.at[h, d - 1], peers[d]
        )

    def placed(h, d, k, band):
        row = z * 4 + (y + 4 - k) % 4 if h == 0 else ((z + 4 - k) % 4) * 4 + y
        local = band - metas[row, 0, 0]
        at = jnp.clip(local, 0, 15)
        block = block_of(h, d)
        piece = first[k][h, block, at] if k else sent[h, (y, z)[h] * 4 + block, at]
        return jnp.where((local >= 0) & (local < 16), piece, jnp.zeros_like(piece))

    def early_block(h, d):
        @pl.loop(0, 32, unroll=4)
        def _(band):
            acc = placed(h, d, 0, band).astype(F32)
            acc = acc + placed(h, d, 2, band).astype(F32)
            kept[h, d, band] = jnp.where(c == 0, acc[0], acc[1])
            early[h, d, band] = jnp.where(c == 0, acc[1], acc[0])

    def gather_block(h, d):
        @pl.loop(0, 32, unroll=4)
        def _(band):
            a = placed(h, d, 1, band)
            b = placed(h, d, 3, band)
            kept[h, d, band] += jnp.where(c == 0, a[0], a[1]).astype(F32) + jnp.where(c == 0, b[0], b[1]).astype(F32)
            other = jnp.where(c == 0, a[1], a[0]).astype(F32) + jnp.where(c == 0, b[1], b[0]).astype(F32)
            leaving[h, d, band] = early[h, d, band] + other

        cross_copy(h, d).start()

    def pass_block(h, d):
        cross_copy(h, d).wait()

        @pl.loop(0, 32, unroll=4)
        def _(band):
            partial[h, d, band] = (kept[h, d, band] + arrived[h, d, band]).astype(BF)

        if d:
            second_copy(h, d).start()

    first_wait(2)
    for d in ORDER:
        for h in range(2):
            early_block(h, d)
    first_wait(1)
    first_wait(3)

    todo = [(h, d) for d in ORDER for h in range(2)]
    for n in range(len(todo) + 2):
        if n < len(todo):
            gather_block(*todo[n])
        if n >= 2:
            pass_block(*todo[n - 2])

    for h in range(2):
        for d in (1, 2, 3):
            second_copy(h, d).wait()

    @pl.loop(0, 16, unroll=2)
    def _(pair):
        lines = [[] for _ in range(4)]
        for odd in range(2):
            band = 2 * pair + odd
            for h in range(2):
                acc = partial[h, 0, band].astype(F32)
                for k in range(3):
                    acc = acc + second[h, k, band].astype(F32)
                for q in range(4):
                    lines[q].append(acc[4 * q : 4 * q + 4])
        for q in range(4):
            quarters[q, pair] = jnp.concatenate(lines[q], axis=0).astype(BF)

    moves = []
    for d in (2, 1, 3):
        cp = remote(quarters.at[(s + d) % 4], planes.at[s], x_send.at[d - 1], x_recv.at[d - 1], xpeers[d])
        cp.start()
        moves.append(cp)
    planes[s] = quarters[s]
    for cp in moves:
        cp.wait()

    top = line < 4
    right = lax.broadcasted_iota(I32, (8, 128), 1) >= 64
    straight = top != (right & (y == 3) & (z == 3))
    for g in range(5):

        @pl.loop(0, 8, unroll=2)
        def _(pair, g=g):
            if g == 0:
                both = planes[0, pair].astype(F32)
            elif g == 4:
                both = planes[3, 8 + pair].astype(F32)
            else:
                both = planes[g, pair].astype(F32) + planes[g - 1, 8 + pair].astype(F32)
            for odd in range(2):
                band = g * 16 + 2 * pair + odd
                under = jnp.where(top, divisor[0, pl.ds(band, 1), :], divisor[1, pl.ds(band, 1), :])
                value = both[8 * odd : 8 * odd + 8] / under
                turned = pltpu.roll(value, 4, 0)
                ready[2 * band] = jnp.where(straight, value, turned)
                ready[2 * band + 1] = jnp.where(straight, turned, value)

    def last_copy(d):
        peer = (e + d) % 32
        return remote(outgoing.at[peer], incoming.at[e], last_send.at[d], last_recv.at[d], {"exp": peer})

    @pl.loop(0, 32)
    def _(d):
        owner = (e + d) % 32
        for t in range(3):
            a = ready[sites[owner * 5 + 2 * t]]
            b = ready[sites[owner * 5 + min(2 * t + 1, 4)]]
            outgoing[owner, t] = jnp.where(top, a, b)

        @pl.when(d > 0)
        def _():
            last_copy(d).start()

    keep = pltpu.make_async_copy(outgoing.at[e], incoming.at[e], own_sem)
    keep.start()

    @pl.loop(1, 32)
    def _(d):
        last_copy(d).wait()

    keep.wait()

    for slot in range(5):
        upper = sites[e * 5 + slot] % 2 == 0
        turned = []
        for blk in range(16):
            parts = []
            for core in range(2):
                a = incoming[exp_index(blk % 4, blk // 4, core), slot // 2]
                b = incoming[exp_index(blk // 4, blk % 4, core), slot // 2]
                v = jnp.where(upper, a, b)
                if core != slot % 2:
                    v = pltpu.roll(v, 4, 0)
                parts.append(v)
            turned.append(pltpu.roll(jnp.where(top, parts[0], parts[1]), 64, 1))
        for blk in range(16):
            out[slot, :, 128 * blk : 128 * blk + 128] = jnp.where(right, turned[blk], turned[blk - 1])


def per_device(images, psf_coef, phases, col_shift, band_offset, exposure_weight, patch_site):
    smem = pl.BlockSpec(memory_space=pltpu.SMEM)
    vmem = pl.BlockSpec(memory_space=pltpu.VMEM)
    dma = pltpu.SemaphoreType.DMA
    return pl.pallas_call(
        coadd_kernel,
        out_shape=jax.ShapeDtypeStruct((5, 8, 2048), F32),
        in_specs=[pl.BlockSpec(memory_space=pl.ANY)] + [smem] * 7,
        out_specs=vmem,
        scratch_shapes=[
            pltpu.VMEM((EXT, COLS), F32),
            pltpu.VMEM((2, 256, 256), BF),
            pltpu.VMEM((4, 128, 160), BF),
            pltpu.VMEM((4, 128, 160), BF),
            pltpu.VMEM((16, 2, EXT, 256), BF),
            pltpu.VMEM((32, 8, 128), I32),
            pltpu.SMEM((16, 8, 128), I32),
            pltpu.VMEM((2, 16, 16, 2, 16, 128), BF),
            pltpu.VMEM((2, 4, 16, 2, 16, 128), BF),
            pltpu.VMEM((2, 4, 16, 2, 16, 128), BF),
            pltpu.VMEM((2, 4, 16, 2, 16, 128), BF),
            pltpu.VMEM((2, 4, 32, 16, 128), F32),
            pltpu.VMEM((2, 4, 32, 16, 128), F32),
            pltpu.VMEM((2, 4, 32, 16, 128), F32),
            pltpu.VMEM((2, 4, 32, 16, 128), F32),
            pltpu.VMEM((2, 4, 32, 16, 128), BF),
            pltpu.VMEM((2, 3, 32, 16, 128), BF),
            pltpu.VMEM((4, 16, 16, 128), BF),
            pltpu.VMEM((4, 16, 16, 128), BF),
            pltpu.VMEM((2, 128, 128), F32),
            pltpu.VMEM((160, 8, 128), F32),
            pltpu.VMEM((32, 3, 8, 128), F32),
            pltpu.VMEM((32, 3, 8, 128), F32),
            dma((4,)), dma((2,)), dma((2,)), dma((7,)), dma((7,)), dma,
            dma((2, 3, 2, 3)), dma((2, 3, 2, 3)), dma((8,)), dma((8,)), dma((2, 3)), dma((2, 3)),
            dma((3,)), dma((3,)), dma((32,)), dma((32,)), dma,
        ],
        compiler_params=pltpu.CompilerParams(
            collective_id=0, has_side_effects=True, vmem_limit_bytes=60 << 20
        ),
        name="coadd",
    )(
        images, psf_coef, phases, jnp.asarray(lanczos_table().reshape(-1)),
        col_shift, band_offset, exposure_weight.astype(F32), patch_site,
    )


def solution(mesh):
    placed = (P("exp", "seg", None), P("exp", None, None), P("exp", None), P("exp"), P("exp"), P("exp"), P())
    return jax.shard_map(per_device, mesh=mesh, in_specs=placed, out_specs=P("exp", "seg", None), check_vma=False)
```

```python
import functools
import numpy as np
import jax
import jax.numpy as jnp
from jax import lax
from jax.experimental import pallas as pl
from jax.experimental.pallas import tpu as pltpu
from jax.sharding import PartitionSpec as P

MESH = pl.DeviceIdType.MESH
BF = jnp.bfloat16
F32 = jnp.float32
I32 = jnp.int32
TAPS = 21
SIGMAS = (1.0, 2.0, 3.5)
HALO = 16
ROWS = 512
COLS = 4096
EXT = ROWS + 2 * HALO


def basis_numbers():
    u = np.arange(TAPS, dtype=np.float64) - TAPS // 2
    out = []
    for s in SIGMAS:
        g = np.exp(-u * u / (2.0 * s * s))
        out.append(g / g.sum())
    return np.stack(out)


def lanczos_table():
    rows = []
    for p in range(16):
        u = np.arange(6, dtype=np.float64) - 2.0 - p / 16.0
        v = np.sinc(u) * np.sinc(u / 3.0)
        rows.append(v / v.sum())
    return np.stack(rows).astype(np.float32)


BASIS = basis_numbers()


def here():
    s = lax.axis_index("seg")
    e = lax.axis_index("exp")
    return s, e // 8, (e // 2) % 4, e % 2


def exp_index(z, y, c):
    return (z * 4 + y) * 2 + c


def banded(shape, distance, numbers):
    out = jnp.zeros(shape, F32)
    for t, number in enumerate(numbers):
        out = jnp.where(distance == t, number, out)
    return out


def split(v):
    high = v.astype(BF)
    return high, (v - high.astype(F32)).astype(BF)


def dot(a, b):
    return jnp.dot(a, b, preferred_element_type=F32)


def exact_dot(a, b):
    return jnp.dot(a, b, precision=lax.Precision.HIGHEST, preferred_element_type=F32)


def taps_of(coef, axis):
    return [
        coef[0, axis, 0] * F32(BASIS[0, t])
        + coef[0, axis, 1] * F32(BASIS[1, t])
        + coef[0, axis, 2] * F32(BASIS[2, t])
        for t in range(TAPS)
    ]


def build_columns(coef, table, phases, shift_ref, cols):
    shift = shift_ref[0]
    kc = taps_of(coef, 1)
    phase = phases[0, 1]
    lz = [table[phase * 6 + n] for n in range(6)]
    k = lax.broadcasted_iota(I32, (256, 256), 0)
    m = lax.broadcasted_iota(I32, (256, 256), 1)
    inner = banded((256, 256), k - m + 10, kc)
    apart = jnp.where((k < 128) == (m < 128), inner, 0.0)
    m = lax.broadcasted_iota(I32, (256, 128), 0)
    j = lax.broadcasted_iota(I32, (256, 128), 1)
    outer = banded((256, 128), m - j - 62 + shift, lz)
    seam = jnp.where((m < 128) == (j < 64), outer, 0.0)
    for variant, (left, right) in enumerate(((inner, outer), (apart, seam))):
        high, low = split(exact_dot(left, right))
        cols[variant, :, 0:128] = high
        cols[variant, :, 128:256] = low


def build_rows(s, coef, table, phases, rhi, rlo, blocks):
    kr = taps_of(coef, 0)
    phase = phases[0, 0]
    lz = [table[phase * 6 + n] for n in range(6)]
    o = lax.broadcasted_iota(I32, (128, 144), 0)
    m = lax.broadcasted_iota(I32, (128, 144), 1)
    row = (o // 32) * 32 + ((o // 4) % 4) * 8 + ((o // 16) % 2) * 4 + o % 4
    outer = banded((128, 144), m - 6 - row, lz)
    m = lax.broadcasted_iota(I32, (144, 160), 0)
    k = lax.broadcasted_iota(I32, (144, 160), 1)
    inner = banded((144, 160), k - m + 2, kr)
    for block in blocks:
        place = s * ROWS + 128 * block - 8 + m
        part = inner if block == 1 else jnp.where((place >= 0) & (place < 4 * ROWS), inner, 0.0)
        high, low = split(exact_dot(outer, part))
        rhi[block] = high
        rlo[block] = low


ORDER = (2, 1, 3, 0)


def coadd_kernel(
    image, coef, phases, table, shift_ref, offset_ref, weight_ref, sites,
    out,
    xf, cols, rhi, rlo, mids, meta, metas, sent, first_1, first_2, first_3, kept, early, leaving, arrived, partial, second,
    quarters, planes, divisor, ready, outgoing, incoming,
    load_sem, halo_send, halo_recv, meta_send, meta_recv, meta_load,
    first_send, first_recv, cross_send, cross_recv, second_send, second_recv,
    x_send, x_recv, last_send, last_recv, own_sem,
):
    s, z, y, c = here()
    e = exp_index(z, y, c)
    chunks = 4
    rows_each = ROWS // chunks
    barrier = pltpu.get_barrier_semaphore()
    xpeers = {d: {"seg": (s + d) % 4} for d in (1, 2, 3)}
    ypeers = {d: {"exp": exp_index(z, (y + d) % 4, c)} for d in (1, 2, 3)}
    zpeers = {d: {"exp": exp_index((z + d) % 4, y, c)} for d in (1, 2, 3)}
    partner = {"exp": exp_index(z, y, 1 - c)}
    near = [peers[d] for peers in (xpeers, ypeers, zpeers) for d in (1, 3, 2)] + [partner]
    for peer in near:
        pl.semaphore_signal(barrier, inc=1, device_id=peer, device_id_type=MESH)

    loads = []
    for i in range(chunks):
        cp = pltpu.make_async_copy(
            image.at[0, pl.ds(i * rows_each, rows_each)],
            xf.at[pl.ds(HALO + i * rows_each, rows_each)],
            load_sem.at[i],
        )
        cp.start()
        loads.append(cp)

    mine = c * 16 + z * 4 + y
    line = lax.broadcasted_iota(I32, (8, 128), 0)
    scaled = (weight_ref[0] * 256.0).astype(I32)
    meta[mine] = jnp.where(line == 0, offset_ref[0], jnp.where(line == 1, shift_ref[0], scaled))

    def remote(src, dst, send, recv, peer):
        return pltpu.make_async_remote_copy(
            src_ref=src, dst_ref=dst, send_sem=send, recv_sem=recv, device_id=peer, device_id_type=MESH
        )

    halos = [
        remote(image.at[0, pl.ds(ROWS - HALO, HALO)], xf.at[pl.ds(0, HALO)],
               halo_send.at[0], halo_recv.at[0], xpeers[1]),
        remote(image.at[0, pl.ds(0, HALO)], xf.at[pl.ds(HALO + ROWS, HALO)],
               halo_send.at[1], halo_recv.at[1], xpeers[3]),
    ]
    build_columns(coef, table, phases, shift_ref, cols)
    pl.semaphore_wait(barrier, len(near))
    for cp in halos:
        cp.start()
    own = meta.at[mine]
    step = [remote(own, own, meta_send.at[d - 1], meta_recv.at[d - 1], ypeers[d]) for d in (1, 2, 3)]
    for cp in step:
        cp.start()
    build_rows(s, coef, table, phases, rhi, rlo, (1,))

    for cp in loads:
        cp.wait()
    weight = weight_ref[0]

    def across(h, jh, fetch):
        first_tile = h * 16 + jh * 2
        high, low = [], []
        for k in range(3):
            tile = (first_tile + k) % 32
            a, b = split(fetch(pl.ds(pl.multiple_of(tile * 128, 128), 128)))
            high.append(a)
            low.append(b)
        parts = []
        for side in range(2):
            variant = jnp.where(first_tile + side == 31, 1, 0)
            a = jnp.concatenate(high[side : side + 2], axis=1)
            b = jnp.concatenate(low[side : side + 2], axis=1)
            both = dot(a, cols[variant])
            cross = dot(b, cols[variant, :, 0:128])
            parts.append(both[:, 0:128] + both[:, 128:256] + cross)
        return split(jnp.concatenate(parts, axis=1))

    def own_rows(h, jh, slot):
        high, low = across(h, jh, lambda tile: xf[HALO : HALO + ROWS, tile])
        mids[slot, 0, HALO : HALO + ROWS, :] = high
        mids[slot, 1, HALO : HALO + ROWS, :] = low

    def edge_fetch(tile):
        above = jnp.where(s > 0, xf[0:HALO, tile], 0.0)
        below = jnp.where(s < 3, xf[HALO + ROWS : EXT, tile], 0.0)
        return jnp.concatenate([above, below], axis=0)

    def edge_rows(h, jh, slot):
        for half, value in enumerate(across(h, jh, edge_fetch)):
            mids[slot, half, 0:HALO, :] = value[0:HALO]
            mids[slot, half, HALO + ROWS : EXT, :] = value[HALO : 2 * HALO]

    def down(h, jh, slot, blocks):
        for block in blocks:
            rows = slice(128 * block, 128 * block + 160)
            a, b = mids[slot, 0, rows, :], mids[slot, 1, rows, :]
            kind = 1 if block in (1, 2) else block
            rh, rl = rhi[kind], rlo[kind]
            got = ((dot(rh, a) + dot(rl, a) + dot(rh, b)) * weight).astype(BF)
            for part in range(2):
                sent[h, jh * 2 + part, 4 * block : 4 * block + 4] = got[
                    :, 128 * part : 128 * part + 128
                ].reshape(4, 2, 16, 128)

    first = {1: first_1, 2: first_2, 3: first_3}
    PIECES = ((4, 8), (0, 4), (12, 4))

    def first_copy(h, d, side, place, piece):
        peers = (ypeers, zpeers)[h]
        bands = pl.ds(*PIECES[piece])
        return remote(
            sent.at[h, pl.ds(place, 2), bands], first[d].at[h, pl.ds(side * 2, 2), bands],
            first_send.at[h, d - 1, side, piece], first_recv.at[h, d - 1, side, piece], peers[d],
        )

    def step_of(h, d, side):
        return (((y, z)[h] + d) % 4) * 2 + side

    for d in (2, 1, 3):

        @pl.loop(0, 2)
        def _(side, d=d):
            for h in range(2):
                jh = step_of(h, d, side)
                slot = h * 8 + jh
                own_rows(h, jh, slot)
                down(h, jh, slot, (1, 2))
                first_copy(h, d, side, jh * 2, 0).start()

    for cp in step:
        cp.wait()
    group = meta.at[pl.ds(c * 16 + z * 4, 4)]
    step = [remote(group, group, meta_send.at[2 + d], meta_recv.at[2 + d], zpeers[d]) for d in (1, 2, 3)]
    for cp in step:
        cp.start()
    build_rows(s, coef, table, phases, rhi, rlo, (0, 3))
    for cp in halos:
        cp.wait()

    for d in (2, 1, 3):

        @pl.loop(0, 2)
        def _(side, d=d):
            for h in range(2):
                jh = step_of(h, d, side)
                slot = h * 8 + jh
                edge_rows(h, jh, slot)
                down(h, jh, slot, (0, 3))
                first_copy(h, d, side, jh * 2, 1).start()
                first_copy(h, d, side, jh * 2, 2).start()

    for cp in step:
        cp.wait()
    half = meta.at[pl.ds(c * 16, 16)]
    metas_copy = pltpu.make_async_copy(half, metas, meta_load)
    metas_copy.start()
    last_meta = remote(half, half, meta_send.at[6], meta_recv.at[6], partner)
    last_meta.start()

    @pl.loop(0, 2)
    def _(side):
        for h in range(2):
            jh = step_of(h, 0, side)
            slot = h * 8 + jh
            own_rows(h, jh, slot)
            edge_rows(h, jh, slot)
            down(h, jh, slot, range(4))

    last_meta.wait()
    metas_copy.wait()

    off = meta[:, 0, :]
    shift = meta[:, 1, :]
    heavy = meta[:, 2, :].astype(F32) * (1.0 / 256.0)
    lane = lax.broadcasted_iota(I32, (32, 128), 1)
    inband = jnp.where((lane >= off) & (lane < off + 64), 1.0, 0.0).T
    for h in range(2):
        block = (4 * y + z, 4 * z + y)[h]
        col = (h * 2048 + block * 128 + 64 + lane) % COLS - shift
        cover = jnp.where((col >= 0) & (col < COLS), heavy, 0.0)
        divisor[h] = jnp.maximum(dot(inband.astype(BF), cover.astype(BF)), 1.0)

    def first_wait(d):
        for h in range(2):
            for side in range(2):
                for piece in range(3):
                    first_copy(h, d, side, 0, piece).wait()

    def block_of(h, d):
        return ((z, y)[h] + d) % 4

    def cross_copy(h, d, half):
        place = (h * 4 + d) * 2 + half
        bands = pl.ds(16 * half, 16)
        return remote(
            leaving.at[h, d, bands], arrived.at[h, d, bands], cross_send.at[place], cross_recv.at[place], partner
        )

    def second_copy(h, d, half):
        peers = (zpeers, ypeers)[h]
        bands = pl.ds(16 * half, 16)
        return remote(
            partial.at[h, d, bands], second.at[h, d - 1, bands],
            second_send.at[h, d - 1, half], second_recv.at[h, d - 1, half], peers[d],
        )

    def placed(h, d, k, band):
        row = z * 4 + (y + 4 - k) % 4 if h == 0 else ((z + 4 - k) % 4) * 4 + y
        local = band - metas[row, 0, 0]
        at = jnp.clip(local, 0, 15)
        block = block_of(h, d)
        piece = first[k][h, block, at] if k else sent[h, (y, z)[h] * 4 + block, at]
        return jnp.where((local >= 0) & (local < 16), piece, jnp.zeros_like(piece))

    def early_block(h, d):
        @pl.loop(0, 32, unroll=4)
        def _(band):
            acc = placed(h, d, 0, band).astype(F32)
            acc = acc + placed(h, d, 2, band).astype(F32)
            kept[h, d, band] = jnp.where(c == 0, acc[0], acc[1])
            early[h, d, band] = jnp.where(c == 0, acc[1], acc[0])

    def gather_block(h, d, half):
        @pl.loop(16 * half, 16 * half + 16, unroll=4)
        def _(band):
            a = placed(h, d, 1, band)
            b = placed(h, d, 3, band)
            kept[h, d, band] += jnp.where(c == 0, a[0], a[1]).astype(F32) + jnp.where(c == 0, b[0], b[1]).astype(F32)
            other = jnp.where(c == 0, a[1], a[0]).astype(F32) + jnp.where(c == 0, b[1], b[0]).astype(F32)
            leaving[h, d, band] = early[h, d, band] + other

        cross_copy(h, d, half).start()

    def pass_block(h, d, half):
        cross_copy(h, d, half).wait()

        @pl.loop(16 * half, 16 * half + 16, unroll=4)
        def _(band):
            partial[h, d, band] = (kept[h, d, band] + arrived[h, d, band]).astype(BF)

        if d:
            second_copy(h, d, half).start()

    first_wait(2)
    for d in ORDER:
        for h in range(2):
            early_block(h, d)
    first_wait(1)
    first_wait(3)

    todo = [(h, d, half) for half in range(2) for d in ORDER for h in range(2)]
    for n in range(len(todo) + 2):
        if n < len(todo):
            gather_block(*todo[n])
        if n >= 2:
            pass_block(*todo[n - 2])

    def x_copy(d, half):
        pairs = pl.ds(8 * half, 8)
        return remote(
            quarters.at[(s + d) % 4, pairs], planes.at[s, pairs],
            x_send.at[d - 1, half], x_recv.at[d - 1, half], xpeers[d],
        )

    for half in range(2):
        for h in range(2):
            for d in (1, 2, 3):
                second_copy(h, d, half).wait()

        @pl.loop(8 * half, 8 * half + 8, unroll=2)
        def _(pair):
            lines = [[] for _ in range(4)]
            for odd in range(2):
                band = 2 * pair + odd
                for h in range(2):
                    acc = partial[h, 0, band].astype(F32)
                    for k in range(3):
                        acc = acc + second[h, k, band].astype(F32)
                    for q in range(4):
                        lines[q].append(acc[4 * q : 4 * q + 4])
            for q in range(4):
                quarters[q, pair] = jnp.concatenate(lines[q], axis=0).astype(BF)

        for d in (2, 1, 3):
            x_copy(d, half).start()
    planes[s] = quarters[s]
    for half in range(2):
        for d in (2, 1, 3):
            x_copy(d, half).wait()

    top = line < 4
    right = lax.broadcasted_iota(I32, (8, 128), 1) >= 64
    straight = top != (right & (y == 3) & (z == 3))
    for g in range(5):

        @pl.loop(0, 8, unroll=2)
        def _(pair, g=g):
            if g == 0:
                both = planes[0, pair].astype(F32)
            elif g == 4:
                both = planes[3, 8 + pair].astype(F32)
            else:
                both = planes[g, pair].astype(F32) + planes[g - 1, 8 + pair].astype(F32)
            for odd in range(2):
                band = g * 16 + 2 * pair + odd
                under = jnp.where(top, divisor[0, pl.ds(band, 1), :], divisor[1, pl.ds(band, 1), :])
                value = both[8 * odd : 8 * odd + 8] / under
                turned = pltpu.roll(value, 4, 0)
                ready[2 * band] = jnp.where(straight, value, turned)
                ready[2 * band + 1] = jnp.where(straight, turned, value)

    def last_copy(d):
        peer = (e + d) % 32
        return remote(outgoing.at[peer], incoming.at[e], last_send.at[d], last_recv.at[d], {"exp": peer})

    @pl.loop(0, 32)
    def _(d):
        owner = (e + d) % 32
        for t in range(3):
            a = ready[sites[owner * 5 + 2 * t]]
            b = ready[sites[owner * 5 + min(2 * t + 1, 4)]]
            outgoing[owner, t] = jnp.where(top, a, b)

        @pl.when(d > 0)
        def _():
            last_copy(d).start()

    keep = pltpu.make_async_copy(outgoing.at[e], incoming.at[e], own_sem)
    keep.start()

    @pl.loop(1, 32)
    def _(d):
        last_copy(d).wait()

    keep.wait()

    for slot in range(5):
        upper = sites[e * 5 + slot] % 2 == 0
        turned = []
        for blk in range(16):
            parts = []
            for core in range(2):
                a = incoming[exp_index(blk % 4, blk // 4, core), slot // 2]
                b = incoming[exp_index(blk // 4, blk % 4, core), slot // 2]
                v = jnp.where(upper, a, b)
                if core != slot % 2:
                    v = pltpu.roll(v, 4, 0)
                parts.append(v)
            turned.append(pltpu.roll(jnp.where(top, parts[0], parts[1]), 64, 1))
        for blk in range(16):
            out[slot, :, 128 * blk : 128 * blk + 128] = jnp.where(right, turned[blk], turned[blk - 1])


def per_device(images, psf_coef, phases, col_shift, band_offset, exposure_weight, patch_site):
    smem = pl.BlockSpec(memory_space=pltpu.SMEM)
    vmem = pl.BlockSpec(memory_space=pltpu.VMEM)
    dma = pltpu.SemaphoreType.DMA
    return pl.pallas_call(
        coadd_kernel,
        out_shape=jax.ShapeDtypeStruct((5, 8, 2048), F32),
        in_specs=[pl.BlockSpec(memory_space=pl.ANY)] + [smem] * 7,
        out_specs=vmem,
        scratch_shapes=[
            pltpu.VMEM((EXT, COLS), F32),
            pltpu.VMEM((2, 256, 256), BF),
            pltpu.VMEM((4, 128, 160), BF),
            pltpu.VMEM((4, 128, 160), BF),
            pltpu.VMEM((16, 2, EXT, 256), BF),
            pltpu.VMEM((32, 8, 128), I32),
            pltpu.SMEM((16, 8, 128), I32),
            pltpu.VMEM((2, 16, 16, 2, 16, 128), BF),
            pltpu.VMEM((2, 4, 16, 2, 16, 128), BF),
            pltpu.VMEM((2, 4, 16, 2, 16, 128), BF),
            pltpu.VMEM((2, 4, 16, 2, 16, 128), BF),
            pltpu.VMEM((2, 4, 32, 16, 128), F32),
            pltpu.VMEM((2, 4, 32, 16, 128), F32),
            pltpu.VMEM((2, 4, 32, 16, 128), F32),
            pltpu.VMEM((2, 4, 32, 16, 128), F32),
            pltpu.VMEM((2, 4, 32, 16, 128), BF),
            pltpu.VMEM((2, 3, 32, 16, 128), BF),
            pltpu.VMEM((4, 16, 16, 128), BF),
            pltpu.VMEM((4, 16, 16, 128), BF),
            pltpu.VMEM((2, 128, 128), F32),
            pltpu.VMEM((160, 8, 128), F32),
            pltpu.VMEM((32, 3, 8, 128), F32),
            pltpu.VMEM((32, 3, 8, 128), F32),
            dma((4,)), dma((2,)), dma((2,)), dma((7,)), dma((7,)), dma,
            dma((2, 3, 2, 3)), dma((2, 3, 2, 3)), dma((16,)), dma((16,)), dma((2, 3, 2)), dma((2, 3, 2)),
            dma((3, 2)), dma((3, 2)), dma((32,)), dma((32,)), dma,
        ],
        compiler_params=pltpu.CompilerParams(
            collective_id=0, has_side_effects=True, vmem_limit_bytes=60 << 20
        ),
        name="coadd",
    )(
        images, psf_coef, phases, jnp.asarray(lanczos_table().reshape(-1)),
        col_shift, band_offset, exposure_weight.astype(F32), patch_site,
    )


def solution(mesh):
    placed = (P("exp", "seg", None), P("exp", None, None), P("exp", None), P("exp"), P("exp"), P("exp"), P())
    return jax.shard_map(per_device, mesh=mesh, in_specs=placed, out_specs=P("exp", "seg", None), check_vma=False)
```

```python
import functools
import numpy as np
import jax
import jax.numpy as jnp
from jax import lax
from jax.experimental import pallas as pl
from jax.experimental.pallas import tpu as pltpu
from jax.sharding import PartitionSpec as P

MESH = pl.DeviceIdType.MESH
BF = jnp.bfloat16
F32 = jnp.float32
I32 = jnp.int32
TAPS = 21
SIGMAS = (1.0, 2.0, 3.5)
HALO = 16
ROWS = 512
COLS = 4096
EXT = ROWS + 2 * HALO


def basis_numbers():
    u = np.arange(TAPS, dtype=np.float64) - TAPS // 2
    out = []
    for s in SIGMAS:
        g = np.exp(-u * u / (2.0 * s * s))
        out.append(g / g.sum())
    return np.stack(out)


def lanczos_table():
    rows = []
    for p in range(16):
        u = np.arange(6, dtype=np.float64) - 2.0 - p / 16.0
        v = np.sinc(u) * np.sinc(u / 3.0)
        rows.append(v / v.sum())
    return np.stack(rows).astype(np.float32)


BASIS = basis_numbers()


def here():
    s = lax.axis_index("seg")
    e = lax.axis_index("exp")
    return s, e // 8, (e // 2) % 4, e % 2


def exp_index(z, y, c):
    return (z * 4 + y) * 2 + c


def banded(shape, distance, numbers):
    out = jnp.zeros(shape, F32)
    for t, number in enumerate(numbers):
        out = jnp.where(distance == t, number, out)
    return out


def split(v):
    high = v.astype(BF)
    return high, (v - high.astype(F32)).astype(BF)


def dot(a, b):
    return jnp.dot(a, b, preferred_element_type=F32)


def exact_dot(a, b):
    return jnp.dot(a, b, precision=lax.Precision.HIGHEST, preferred_element_type=F32)


def taps_of(coef, axis):
    return [
        coef[0, axis, 0] * F32(BASIS[0, t])
        + coef[0, axis, 1] * F32(BASIS[1, t])
        + coef[0, axis, 2] * F32(BASIS[2, t])
        for t in range(TAPS)
    ]


def build_columns(coef, table, phases, shift_ref, cols):
    shift = shift_ref[0]
    kc = taps_of(coef, 1)
    phase = phases[0, 1]
    lz = [table[phase * 6 + n] for n in range(6)]
    k = lax.broadcasted_iota(I32, (256, 256), 0)
    m = lax.broadcasted_iota(I32, (256, 256), 1)
    inner = banded((256, 256), k - m + 10, kc)
    apart = jnp.where((k < 128) == (m < 128), inner, 0.0)
    m = lax.broadcasted_iota(I32, (256, 128), 0)
    j = lax.broadcasted_iota(I32, (256, 128), 1)
    outer = banded((256, 128), m - j - 62 + shift, lz)
    seam = jnp.where((m < 128) == (j < 64), outer, 0.0)
    for variant, (left, right) in enumerate(((inner, outer), (apart, seam))):
        high, low = split(exact_dot(left, right))
        cols[variant, :, 0:128] = high
        cols[variant, :, 128:256] = low


def build_rows(s, coef, table, phases, rhi, rlo, blocks):
    kr = taps_of(coef, 0)
    phase = phases[0, 0]
    lz = [table[phase * 6 + n] for n in range(6)]
    o = lax.broadcasted_iota(I32, (128, 144), 0)
    m = lax.broadcasted_iota(I32, (128, 144), 1)
    row = (o // 32) * 32 + ((o // 4) % 4) * 8 + ((o // 16) % 2) * 4 + o % 4
    outer = banded((128, 144), m - 6 - row, lz)
    m = lax.broadcasted_iota(I32, (144, 160), 0)
    k = lax.broadcasted_iota(I32, (144, 160), 1)
    inner = banded((144, 160), k - m + 2, kr)
    for block in blocks:
        place = s * ROWS + 128 * block - 8 + m
        part = inner if block == 1 else jnp.where((place >= 0) & (place < 4 * ROWS), inner, 0.0)
        high, low = split(exact_dot(outer, part))
        rhi[block] = high
        rlo[block] = low


ORDER = (2, 1, 3, 0)


def coadd_kernel(
    image, coef, phases, table, shift_ref, offset_ref, weight_ref, sites,
    out,
    xf, cols, rhi, rlo, mids, meta, metas, sent, first_1, first_2, first_3, kept, early, leaving, arrived, partial, second,
    quarters, planes, divisor, ready, outgoing, incoming,
    load_sem, halo_send, halo_recv, meta_send, meta_recv, meta_load,
    first_send, first_recv, cross_send, cross_recv, second_send, second_recv,
    x_send, x_recv, last_send, last_recv, own_sem,
):
    s, z, y, c = here()
    e = exp_index(z, y, c)
    chunks = 4
    rows_each = ROWS // chunks
    barrier = pltpu.get_barrier_semaphore()
    xpeers = {d: {"seg": (s + d) % 4} for d in (1, 2, 3)}
    ypeers = {d: {"exp": exp_index(z, (y + d) % 4, c)} for d in (1, 2, 3)}
    zpeers = {d: {"exp": exp_index((z + d) % 4, y, c)} for d in (1, 2, 3)}
    partner = {"exp": exp_index(z, y, 1 - c)}
    near = [peers[d] for peers in (xpeers, ypeers, zpeers) for d in (1, 3, 2)] + [partner]
    for peer in near:
        pl.semaphore_signal(barrier, inc=1, device_id=peer, device_id_type=MESH)

    loads = []
    for i in range(chunks):
        cp = pltpu.make_async_copy(
            image.at[0, pl.ds(i * rows_each, rows_each)],
            xf.at[pl.ds(HALO + i * rows_each, rows_each)],
            load_sem.at[i],
        )
        cp.start()
        loads.append(cp)

    mine = c * 16 + z * 4 + y
    line = lax.broadcasted_iota(I32, (8, 128), 0)
    scaled = (weight_ref[0] * 256.0).astype(I32)
    meta[mine] = jnp.where(line == 0, offset_ref[0], jnp.where(line == 1, shift_ref[0], scaled))

    def remote(src, dst, send, recv, peer):
        return pltpu.make_async_remote_copy(
            src_ref=src, dst_ref=dst, send_sem=send, recv_sem=recv, device_id=peer, device_id_type=MESH
        )

    halos = [
        remote(image.at[0, pl.ds(ROWS - HALO, HALO)], xf.at[pl.ds(0, HALO)],
               halo_send.at[0], halo_recv.at[0], xpeers[1]),
        remote(image.at[0, pl.ds(0, HALO)], xf.at[pl.ds(HALO + ROWS, HALO)],
               halo_send.at[1], halo_recv.at[1], xpeers[3]),
    ]
    build_columns(coef, table, phases, shift_ref, cols)
    pl.semaphore_wait(barrier, len(near))
    for cp in halos:
        cp.start()
    own = meta.at[mine]
    step = [remote(own, own, meta_send.at[d - 1], meta_recv.at[d - 1], ypeers[d]) for d in (1, 2, 3)]
    for cp in step:
        cp.start()
    build_rows(s, coef, table, phases, rhi, rlo, (1,))

    for cp in loads:
        cp.wait()
    weight = weight_ref[0]

    def across(h, jh, fetch):
        first_tile = h * 16 + jh * 2
        high, low = [], []
        for k in range(3):
            tile = (first_tile + k) % 32
            a, b = split(fetch(pl.ds(pl.multiple_of(tile * 128, 128), 128)))
            high.append(a)
            low.append(b)
        parts = []
        for side in range(2):
            variant = jnp.where(first_tile + side == 31, 1, 0)
            a = jnp.concatenate(high[side : side + 2], axis=1)
            b = jnp.concatenate(low[side : side + 2], axis=1)
            both = dot(a, cols[variant])
            cross = dot(b, cols[variant, :, 0:128])
            parts.append(both[:, 0:128] + both[:, 128:256] + cross)
        return split(jnp.concatenate(parts, axis=1))

    def own_rows(h, jh, slot):
        high, low = across(h, jh, lambda tile: xf[HALO : HALO + ROWS, tile])
        mids[slot, 0, HALO : HALO + ROWS, :] = high
        mids[slot, 1, HALO : HALO + ROWS, :] = low

    def edge_fetch(tile):
        above = jnp.where(s > 0, xf[0:HALO, tile], 0.0)
        below = jnp.where(s < 3, xf[HALO + ROWS : EXT, tile], 0.0)
        return jnp.concatenate([above, below], axis=0)

    def edge_rows(h, jh, slot):
        for half, value in enumerate(across(h, jh, edge_fetch)):
            mids[slot, half, 0:HALO, :] = value[0:HALO]
            mids[slot, half, HALO + ROWS : EXT, :] = value[HALO : 2 * HALO]

    def down(h, jh, slot, blocks):
        for block in blocks:
            rows = slice(128 * block, 128 * block + 160)
            a, b = mids[slot, 0, rows, :], mids[slot, 1, rows, :]
            kind = 1 if block in (1, 2) else block
            rh, rl = rhi[kind], rlo[kind]
            got = ((dot(rh, a) + dot(rl, a) + dot(rh, b)) * weight).astype(BF)
            for part in range(2):
                sent[h, jh * 2 + part, 4 * block : 4 * block + 4] = got[
                    :, 128 * part : 128 * part + 128
                ].reshape(4, 2, 16, 128)

    first = {1: first_1, 2: first_2, 3: first_3}
    PIECES = ((4, 8), (0, 4), (12, 4))

    def first_copy(h, d, side, place, piece):
        peers = (ypeers, zpeers)[h]
        bands = pl.ds(*PIECES[piece])
        return remote(
            sent.at[h, pl.ds(place, 2), bands], first[d].at[h, pl.ds(side * 2, 2), bands],
            first_send.at[h, d - 1, side, piece], first_recv.at[h, d - 1, side, piece], peers[d],
        )

    def step_of(h, d, side):
        return (((y, z)[h] + d) % 4) * 2 + side

    for d in (2, 1, 3):

        @pl.loop(0, 2)
        def _(side, d=d):
            for h in range(2):
                jh = step_of(h, d, side)
                slot = h * 8 + jh
                own_rows(h, jh, slot)
                down(h, jh, slot, (1, 2))
                first_copy(h, d, side, jh * 2, 0).start()

    for cp in step:
        cp.wait()
    group = meta.at[pl.ds(c * 16 + z * 4, 4)]
    step = [remote(group, group, meta_send.at[2 + d], meta_recv.at[2 + d], zpeers[d]) for d in (1, 2, 3)]
    for cp in step:
        cp.start()
    build_rows(s, coef, table, phases, rhi, rlo, (0, 3))
    for cp in halos:
        cp.wait()

    for d in (2, 1, 3):

        @pl.loop(0, 2)
        def _(side, d=d):
            for h in range(2):
                jh = step_of(h, d, side)
                slot = h * 8 + jh
                edge_rows(h, jh, slot)
                down(h, jh, slot, (0, 3))
                first_copy(h, d, side, jh * 2, 1).start()
                first_copy(h, d, side, jh * 2, 2).start()

    for cp in step:
        cp.wait()
    half = meta.at[pl.ds(c * 16, 16)]
    metas_copy = pltpu.make_async_copy(half, metas, meta_load)
    metas_copy.start()
    last_meta = remote(half, half, meta_send.at[6], meta_recv.at[6], partner)
    last_meta.start()

    @pl.loop(0, 2)
    def _(side):
        for h in range(2):
            jh = step_of(h, 0, side)
            slot = h * 8 + jh
            own_rows(h, jh, slot)
            edge_rows(h, jh, slot)
            down(h, jh, slot, range(4))

    last_meta.wait()
    metas_copy.wait()

    off = meta[:, 0, :]
    shift = meta[:, 1, :]
    heavy = meta[:, 2, :].astype(F32) * (1.0 / 256.0)
    lane = lax.broadcasted_iota(I32, (32, 128), 1)
    inband = jnp.where((lane >= off) & (lane < off + 64), 1.0, 0.0).T
    for h in range(2):
        block = (4 * y + z, 4 * z + y)[h]
        col = (h * 2048 + block * 128 + 64 + lane) % COLS - shift
        cover = jnp.where((col >= 0) & (col < COLS), heavy, 0.0)
        divisor[h] = jnp.maximum(dot(inband.astype(BF), cover.astype(BF)), 1.0)

    def first_wait(d):
        for h in range(2):
            for side in range(2):
                for piece in range(3):
                    first_copy(h, d, side, 0, piece).wait()

    def block_of(h, d):
        return ((z, y)[h] + d) % 4

    def cross_copy(h, d, half):
        place = (h * 4 + d) * 2 + half
        bands = pl.ds(16 * half, 16)
        return remote(
            leaving.at[h, d, bands], arrived.at[h, d, bands], cross_send.at[place], cross_recv.at[place], partner
        )

    def second_copy(h, d, half):
        peers = (zpeers, ypeers)[h]
        bands = pl.ds(16 * half, 16)
        return remote(
            partial.at[h, d, bands], second.at[h, d - 1, bands],
            second_send.at[h, d - 1, half], second_recv.at[h, d - 1, half], peers[d],
        )

    def placed(h, d, k, band):
        row = z * 4 + (y + 4 - k) % 4 if h == 0 else ((z + 4 - k) % 4) * 4 + y
        local = band - metas[row, 0, 0]
        at = jnp.clip(local, 0, 15)
        block = block_of(h, d)
        piece = first[k][h, block, at] if k else sent[h, (y, z)[h] * 4 + block, at]
        return jnp.where((local >= 0) & (local < 16), piece, jnp.zeros_like(piece))

    def early_block(h, d):
        @pl.loop(0, 32, unroll=4)
        def _(band):
            acc = placed(h, d, 0, band).astype(F32)
            acc = acc + placed(h, d, 2, band).astype(F32)
            kept[h, d, band] = jnp.where(c == 0, acc[0], acc[1])
            early[h, d, band] = jnp.where(c == 0, acc[1], acc[0])

    def gather_block(h, d, half):
        @pl.loop(16 * half, 16 * half + 16, unroll=4)
        def _(band):
            a = placed(h, d, 1, band)
            b = placed(h, d, 3, band)
            kept[h, d, band] += jnp.where(c == 0, a[0], a[1]).astype(F32) + jnp.where(c == 0, b[0], b[1]).astype(F32)
            other = jnp.where(c == 0, a[1], a[0]).astype(F32) + jnp.where(c == 0, b[1], b[0]).astype(F32)
            leaving[h, d, band] = early[h, d, band] + other

        cross_copy(h, d, half).start()

    def pass_block(h, d, half):
        cross_copy(h, d, half).wait()

        @pl.loop(16 * half, 16 * half + 16, unroll=4)
        def _(band):
            partial[h, d, band] = (kept[h, d, band] + arrived[h, d, band]).astype(BF)

        if d:
            second_copy(h, d, half).start()

    first_wait(2)
    for d in ORDER:
        for h in range(2):
            early_block(h, d)
    first_wait(1)
    first_wait(3)

    todo = [(h, d, half) for half in range(2) for d in ORDER for h in range(2)]
    for n in range(len(todo) + 4):
        if n < len(todo):
            gather_block(*todo[n])
        if n >= 4:
            pass_block(*todo[n - 4])

    def x_copy(d, half):
        pairs = pl.ds(8 * half, 8)
        return remote(
            quarters.at[(s + d) % 4, pairs], planes.at[s, pairs],
            x_send.at[d - 1, half], x_recv.at[d - 1, half], xpeers[d],
        )

    for half in range(2):
        for h in range(2):
            for d in (1, 2, 3):
                second_copy(h, d, half).wait()

        @pl.loop(8 * half, 8 * half + 8, unroll=2)
        def _(pair):
            lines = [[] for _ in range(4)]
            for odd in range(2):
                band = 2 * pair + odd
                for h in range(2):
                    acc = partial[h, 0, band].astype(F32)
                    for k in range(3):
                        acc = acc + second[h, k, band].astype(F32)
                    for q in range(4):
                        lines[q].append(acc[4 * q : 4 * q + 4])
            for q in range(4):
                quarters[q, pair] = jnp.concatenate(lines[q], axis=0).astype(BF)

        for d in (2, 1, 3):
            x_copy(d, half).start()
    planes[s] = quarters[s]
    for half in range(2):
        for d in (2, 1, 3):
            x_copy(d, half).wait()

    top = line < 4
    right = lax.broadcasted_iota(I32, (8, 128), 1) >= 64
    straight = top != (right & (y == 3) & (z == 3))
    for g in range(5):

        @pl.loop(0, 8, unroll=2)
        def _(pair, g=g):
            if g == 0:
                both = planes[0, pair].astype(F32)
            elif g == 4:
                both = planes[3, 8 + pair].astype(F32)
            else:
                both = planes[g, pair].astype(F32) + planes[g - 1, 8 + pair].astype(F32)
            for odd in range(2):
                band = g * 16 + 2 * pair + odd
                under = jnp.where(top, divisor[0, pl.ds(band, 1), :], divisor[1, pl.ds(band, 1), :])
                value = both[8 * odd : 8 * odd + 8] / under
                turned = pltpu.roll(value, 4, 0)
                ready[2 * band] = jnp.where(straight, value, turned)
                ready[2 * band + 1] = jnp.where(straight, turned, value)

    def last_copy(d):
        peer = (e + d) % 32
        return remote(outgoing.at[peer], incoming.at[e], last_send.at[d], last_recv.at[d], {"exp": peer})

    @pl.loop(0, 32)
    def _(d):
        owner = (e + d) % 32
        for t in range(3):
            a = ready[sites[owner * 5 + 2 * t]]
            b = ready[sites[owner * 5 + min(2 * t + 1, 4)]]
            outgoing[owner, t] = jnp.where(top, a, b)

        @pl.when(d > 0)
        def _():
            last_copy(d).start()

    keep = pltpu.make_async_copy(outgoing.at[e], incoming.at[e], own_sem)
    keep.start()

    @pl.loop(1, 32)
    def _(d):
        last_copy(d).wait()

    keep.wait()

    for slot in range(5):
        upper = sites[e * 5 + slot] % 2 == 0
        turned = []
        for blk in range(16):
            parts = []
            for core in range(2):
                a = incoming[exp_index(blk % 4, blk // 4, core), slot // 2]
                b = incoming[exp_index(blk // 4, blk % 4, core), slot // 2]
                v = jnp.where(upper, a, b)
                if core != slot % 2:
                    v = pltpu.roll(v, 4, 0)
                parts.append(v)
            turned.append(pltpu.roll(jnp.where(top, parts[0], parts[1]), 64, 1))
        for blk in range(16):
            out[slot, :, 128 * blk : 128 * blk + 128] = jnp.where(right, turned[blk], turned[blk - 1])


def per_device(images, psf_coef, phases, col_shift, band_offset, exposure_weight, patch_site):
    smem = pl.BlockSpec(memory_space=pltpu.SMEM)
    vmem = pl.BlockSpec(memory_space=pltpu.VMEM)
    dma = pltpu.SemaphoreType.DMA
    return pl.pallas_call(
        coadd_kernel,
        out_shape=jax.ShapeDtypeStruct((5, 8, 2048), F32),
        in_specs=[pl.BlockSpec(memory_space=pl.ANY)] + [smem] * 7,
        out_specs=vmem,
        scratch_shapes=[
            pltpu.VMEM((EXT, COLS), F32),
            pltpu.VMEM((2, 256, 256), BF),
            pltpu.VMEM((4, 128, 160), BF),
            pltpu.VMEM((4, 128, 160), BF),
            pltpu.VMEM((16, 2, EXT, 256), BF),
            pltpu.VMEM((32, 8, 128), I32),
            pltpu.SMEM((16, 8, 128), I32),
            pltpu.VMEM((2, 16, 16, 2, 16, 128), BF),
            pltpu.VMEM((2, 4, 16, 2, 16, 128), BF),
            pltpu.VMEM((2, 4, 16, 2, 16, 128), BF),
            pltpu.VMEM((2, 4, 16, 2, 16, 128), BF),
            pltpu.VMEM((2, 4, 32, 16, 128), F32),
            pltpu.VMEM((2, 4, 32, 16, 128), F32),
            pltpu.VMEM((2, 4, 32, 16, 128), F32),
            pltpu.VMEM((2, 4, 32, 16, 128), F32),
            pltpu.VMEM((2, 4, 32, 16, 128), BF),
            pltpu.VMEM((2, 3, 32, 16, 128), BF),
            pltpu.VMEM((4, 16, 16, 128), BF),
            pltpu.VMEM((4, 16, 16, 128), BF),
            pltpu.VMEM((2, 128, 128), F32),
            pltpu.VMEM((160, 8, 128), F32),
            pltpu.VMEM((32, 3, 8, 128), F32),
            pltpu.VMEM((32, 3, 8, 128), F32),
            dma((4,)), dma((2,)), dma((2,)), dma((7,)), dma((7,)), dma,
            dma((2, 3, 2, 3)), dma((2, 3, 2, 3)), dma((16,)), dma((16,)), dma((2, 3, 2)), dma((2, 3, 2)),
            dma((3, 2)), dma((3, 2)), dma((32,)), dma((32,)), dma,
        ],
        compiler_params=pltpu.CompilerParams(
            collective_id=0, has_side_effects=True, vmem_limit_bytes=60 << 20
        ),
        name="coadd",
    )(
        images, psf_coef, phases, jnp.asarray(lanczos_table().reshape(-1)),
        col_shift, band_offset, exposure_weight.astype(F32), patch_site,
    )


def solution(mesh):
    placed = (P("exp", "seg", None), P("exp", None, None), P("exp", None), P("exp"), P("exp"), P("exp"), P())
    return jax.shard_map(per_device, mesh=mesh, in_specs=placed, out_specs=P("exp", "seg", None), check_vma=False)
```
